256 devices in a mesh: ctx: 16 (over z_lo, y, core), uly: 16 (over x, z_hi).
Axes of the slice: x: 4, y: 4, z: 8 (z_hi: 4, z_lo: 2; z = z_hi * 2 + z_lo), core: 2. Of those that a mesh axis runs over, the one named last changes fastest.
Arguments:
- query: bfloat16 [32768, 5120], P(('ctx', 'uly')), may hold values from -8 to 8
- key: bfloat16 [32768, 5120], P(('ctx', 'uly')), may hold values from -8 to 8
- value: bfloat16 [32768, 5120], P(('ctx', 'uly')), may hold values from -6 to 6
- dout: bfloat16 [32768, 5120], P(('ctx', 'uly')), may hold values from -6 to 6
- tile_mask: int32 [40, 256, 5], replicated, may hold values from 0 to 1, as said below
Outputs:
- grad_query: bfloat16 [32768, 5120], P(('ctx', 'uly'))
- grad_key: bfloat16 [32768, 5120], P(('ctx', 'uly'))
- grad_value: bfloat16 [32768, 5120], P(('ctx', 'uly'))
The draws below stay inside these ranges and needn't reach their ends.
Inputs may be any that keep to these rules, and one draw needn't show every extreme that they name: `tile_mask`: the tile of a block with itself (offset 2) is active for every head and block.
All inputs are finite; a program needn't handle non-finite values.
Results may differ from the reference program's by a relative error of at most 0.0053.
Values may be sent and summed in bfloat16 or wider, within the bound.
No kernel may reach another device: no remote copies, remote signals or barrier semaphores. Data moves between devices by JAX's collectives and lax.ppermute only.
A program may use at most 128 MiB of HBM per device.

```python
import math
import jax
import jax.numpy as jnp
from jax import lax

H = 40
HD = 128
D = 5120
BLK = 128
W = 2
TOKENS = 32768


def draw_query(key, part):
    noise = jax.random.normal(jax.random.fold_in(key, 1), (TOKENS, H * HD), jnp.float32)
    return jnp.clip(noise, -6.0, 6.0).astype(jnp.bfloat16)


def draw_key(key, part):
    noise = jax.random.normal(jax.random.fold_in(key, 2), (TOKENS, H * HD), jnp.float32)
    return jnp.clip(noise, -6.0, 6.0).astype(jnp.bfloat16)


def draw_tile_mask(key, part):
    density = jax.random.randint(jax.random.fold_in(key, 1), (H, 1, 1), 3, 11)
    tile_rolls = jax.random.randint(jax.random.fold_in(key, 2), (H, TOKENS // BLK, 2 * W + 1), 0, 10)
    tile_draw = (tile_rolls < density).astype(jnp.int32)
    on_diagonal = jnp.arange(2 * W + 1) == W
    return jnp.where(on_diagonal[None, None, :], 1, tile_draw).astype(jnp.int32)


def block_scale(own_key, shape, split, low, high):
    loudness = 1.0
    for position, parts in split:
        heights = jax.random.uniform(jax.random.fold_in(jax.random.fold_in(own_key, 6), position), (parts,), jnp.float32, low / len(split), high / len(split))
        loudness = loudness * jnp.repeat(jnp.exp(heights), shape[position] // parts).reshape((-1,) + (1,) * (len(shape) - 1 - position))
    return loudness


def scatter_about(stream_key, shape, width, reach, pieces=(), held_as=jnp.bfloat16):
    values = width * jax.random.normal(stream_key, shape, jnp.float32)
    if pieces:
        values = values * block_scale(stream_key, shape, pieces, -0.22, 0.18)
    return jnp.clip(values, -reach, reach).astype(held_as)


def setup_inputs(seed: int = 0) -> dict:
    arg_keys = jax.random.split(jax.random.key(seed), 6)
    return {
        "query": draw_query(jax.random.fold_in(arg_keys[5], 71), 0),
        "key": draw_key(jax.random.fold_in(arg_keys[5], 71), 0),
        "value": scatter_about(arg_keys[2], (TOKENS, D), 1.0, 6.0, ((0, 256),)),
        "dout": scatter_about(arg_keys[3], (TOKENS, D), 1.0, 6.0, ((0, 256),)),
        "tile_mask": draw_tile_mask(jax.random.fold_in(arg_keys[5], 71), 0),
    }


def window_stack(blocks, block_count, tile_span):
    return jnp.stack([blocks[offset:offset + block_count] for offset in range(tile_span)], 1)

def attend_grad(query_matrix, key_ext, value_ext, output_gradient, active, logit_scale):
    block_count = query_matrix.shape[0]
    tile_span = active.shape[1]
    query_matrix = query_matrix.astype(jnp.float32)
    output_gradient = output_gradient.astype(jnp.float32)
    windowed_keys = window_stack(key_ext.astype(jnp.float32), block_count, tile_span)
    windowed_values = window_stack(value_ext.astype(jnp.float32), block_count, tile_span)
    attention_logits = jnp.einsum('mip,mejp->meij', query_matrix, windowed_keys) * logit_scale
    masked = jnp.where(active[:, :, None, None], attention_logits, -jnp.inf)
    row_top = lax.optimization_barrier(jnp.max(masked, axis=(1, 3), keepdims=True))
    weights = jnp.exp(masked - row_top)
    denom_sum = lax.optimization_barrier(jnp.sum(weights, axis=(1, 3), keepdims=True))
    prob_f = weights / denom_sum
    backward_probability = lax.optimization_barrier(prob_f.astype(jnp.bfloat16)).astype(jnp.float32)
    probability_gradient = jnp.einsum('mip,mejp->meij', output_gradient, windowed_values)
    row_delta = lax.optimization_barrier(jnp.sum(prob_f * probability_gradient, axis=(1, 3), keepdims=True))
    score_gradient = lax.optimization_barrier((prob_f * (probability_gradient - row_delta)).astype(jnp.bfloat16)).astype(jnp.float32)
    query_gradient_rows = jnp.einsum('luar,lurs->las', score_gradient, windowed_keys) * logit_scale
    windowed_key_gradient = jnp.einsum('gxin,gie->gxne', score_gradient, query_matrix) * logit_scale
    windowed_value_gradient = jnp.einsum('gxin,gie->gxne', backward_probability, output_gradient)
    key_grad = sum((jnp.pad(windowed_key_gradient[:, offset], ((offset, tile_span - 1 - offset), (0, 0), (0, 0))) for offset in range(tile_span)))
    value_grad = sum((jnp.pad(windowed_value_gradient[:, offset], ((offset, tile_span - 1 - offset), (0, 0), (0, 0))) for offset in range(tile_span)))
    return (query_gradient_rows, key_grad, value_grad)

def reference(query, key, value, dout, tile_mask):
    n_tokens, model_width = query.shape
    n_heads = tile_mask.shape[0]
    head_dim = model_width // n_heads
    tile_span = tile_mask.shape[2]
    reach_blocks = tile_span // 2
    all_blocks = n_tokens // BLK
    logit_scale = 1.0 / math.sqrt(head_dim)
    offsets = jnp.arange(tile_span, dtype=jnp.int32) - reach_blocks
    key_block = jnp.arange(all_blocks, dtype=jnp.int32)[:, None] + offsets[None, :]
    key_ok = (key_block >= 0) & (key_block < all_blocks)
    edge_pad = ((reach_blocks, reach_blocks), (0, 0), (0, 0))

    def per_head(head_index):

        def columns(source):
            part_cols = lax.dynamic_slice_in_dim(source, head_index * head_dim, head_dim, 1)
            return part_cols.reshape(all_blocks, BLK, head_dim)
        mask_head = lax.dynamic_index_in_dim(tile_mask, head_index, 0, keepdims=False)
        active = (mask_head != 0) & key_ok
        query_gradient_rows, key_grad, value_grad = attend_grad(columns(query), jnp.pad(columns(key), edge_pad), jnp.pad(columns(value), edge_pad), columns(dout), active, logit_scale)
        inner = slice(reach_blocks, reach_blocks + all_blocks)
        return (query_gradient_rows.astype(jnp.bfloat16).reshape(n_tokens, head_dim), key_grad[inner].astype(jnp.bfloat16).reshape(n_tokens, head_dim), value_grad[inner].astype(jnp.bfloat16).reshape(n_tokens, head_dim))
    grads = lax.map(per_head, jnp.arange(n_heads, dtype=jnp.int32))

    def to_tokens(stacked):
        return jnp.transpose(stacked, (1, 0, 2)).reshape(n_tokens, model_width)
    return (to_tokens(grads[0]), to_tokens(grads[1]), to_tokens(grads[2]))
```

```python
import math

import jax
import jax.numpy as jnp
from jax import lax
from jax.experimental import pallas as pl
from jax.experimental.pallas import tpu as pltpu
from jax.sharding import PartitionSpec as P


BLK = 128
HD = 128
NZ = 4
CHUNKS = ((0, 6), (6, 4))
CW = 256
SCALE = 1.0 / math.sqrt(HD)
EXP2_SCALE = SCALE / math.log(2.0)
BF = jnp.bfloat16
F32 = jnp.float32


MIB = 1 << 20


def grant(mib):
    return pltpu.CompilerParams(vmem_limit_bytes=mib * MIB)


def cost(flops, nbytes):
    return pl.CostEstimate(flops=flops, bytes_accessed=nbytes, transcendentals=0)


def pack_body(zh, a1, a2, a3, b1, b2, b3, o1, o2, o3):
    for a, b, o in ((a1, b1, o1), (a2, b2, o2), (a3, b3, o3)):
        o[0] = a[...]
        o[1] = b[...]


def pack(zh, a, b, first, heads, group):
    per, off, steps = group * HD // CW, first * HD // CW, heads * HD // CW

    def src(s):
        return pl.BlockSpec((BLK, CW), lambda i, z: (0, lax.rem(z[0] + s, NZ) * per + off + i))

    out = pl.BlockSpec((2, BLK, CW), lambda i, z: (0, 0, i))
    n = heads * HD
    return pl.pallas_call(
        pack_body,
        grid_spec=pltpu.PrefetchScalarGridSpec(
            num_scalar_prefetch=1,
            grid=(steps,),
            in_specs=[src(1), src(2), src(3), src(1), src(2), src(3)],
            out_specs=[out, out, out],
        ),
        out_shape=[jax.ShapeDtypeStruct((2, BLK, n), BF)] * 3,
        cost_estimate=cost(0, 12 * BLK * n * 2),
        compiler_params=grant(8),
    )(zh, a, a, a, b, b, b)


def unpack_body(zh, k, v, r1, r2, r3, lo, hi):
    z = zh[0]
    for s, (kk, vv) in enumerate(((k, v), (r1.at[0], r1.at[1]), (r2.at[0], r2.at[1]), (r3.at[0], r3.at[1]))):
        b = lax.rem(z + NZ - s, NZ)

        @pl.when(b < 2)
        def _():
            lo[b, 0] = kk[...]
            lo[b, 1] = vv[...]

        @pl.when(b >= 2)
        def _():
            hi[b - 2, 0] = kk[...]
            hi[b - 2, 1] = vv[...]


def unpack(zh, k, v, recv, group):
    n = group * HD
    per = n // CW
    own = pl.BlockSpec((BLK, CW), lambda i, z: (0, z[0] * per + i))
    got = pl.BlockSpec((2, BLK, CW), lambda i, z: (0, 0, i))
    half = pl.BlockSpec((2, 2, BLK, CW), lambda i, z: (0, 0, 0, i))
    return pl.pallas_call(
        unpack_body,
        grid_spec=pltpu.PrefetchScalarGridSpec(
            num_scalar_prefetch=1, grid=(per,), in_specs=[own, own, got, got, got], out_specs=[half, half]
        ),
        out_shape=[jax.ShapeDtypeStruct((2, 2, BLK, n), BF)] * 2,
        cost_estimate=cost(0, 16 * BLK * n * 2),
        compiler_params=grant(10),
        name="unpack",
    )(zh, k, v, *recv)


def attend_body(zh, q0, g0, x1, x2, x3, before, lo, hi, after, bias,
                dq0, dq1, dq2, dq3, rim_before, rim_after, own,
                qs, gs, ks, vs, dqs, dk, dv):
    z = zh[0]
    for s, (qq, gg) in enumerate(((q0, g0), (x1.at[0], x1.at[1]), (x2.at[0], x2.at[1]), (x3.at[0], x3.at[1]))):
        row = pl.multiple_of(lax.rem(z + NZ - s, NZ) * BLK, BLK)
        qs[pl.ds(row, BLK), :] = qq[...]
        gs[pl.ds(row, BLK), :] = gg[...]
    for i, (ref, j) in enumerate(
        ((before, 0), (before, 1), (lo, 0), (lo, 1), (hi, 0), (hi, 1), (after, 0), (after, 1))
    ):
        ks[i * BLK : (i + 1) * BLK, :] = ref[j, 0]
        vs[i * BLK : (i + 1) * BLK, :] = ref[j, 1]
    nt = (((1,), (1,)), ((), ()))
    tn = (((0,), (0,)), ((), ()))
    nn = (((1,), (0,)), ((), ()))
    for pair in range(2):
        r0 = pair * 2 * BLK
        kw, vw = ks[r0 : r0 + 6 * BLK, :], vs[r0 : r0 + 6 * BLK, :]
        q, g = qs[r0 : r0 + 2 * BLK, :], gs[r0 : r0 + 2 * BLK, :]
        st = lax.dot_general(kw, q, nt, preferred_element_type=F32)
        st = st.reshape(6, BLK, 2 * BLK) + bias[0, pair][:, None, :]
        top = jnp.max(jnp.max(st, axis=0), axis=0, keepdims=True)[None]
        e = jnp.exp2((st - top) * EXP2_SCALE)
        total = jnp.sum(jnp.sum(e, axis=0), axis=0, keepdims=True)[None]
        p = e * (1.0 / total)
        dp = lax.dot_general(vw, g, nt, preferred_element_type=F32).reshape(6, BLK, 2 * BLK)
        delta = jnp.sum(jnp.sum(p * dp, axis=0), axis=0, keepdims=True)[None]
        ds = (p * (dp - delta)).astype(BF).reshape(6 * BLK, 2 * BLK)
        pb = p.astype(BF).reshape(6 * BLK, 2 * BLK)
        dvw = lax.dot_general(pb, g, nn, preferred_element_type=F32)
        dkw = lax.dot_general(ds, q, nn, preferred_element_type=F32)
        dqw = lax.dot_general(ds, kw, tn, preferred_element_type=F32) * SCALE
        dqs[2 * pair] = dqw[:BLK].astype(BF)
        dqs[2 * pair + 1] = dqw[BLK:].astype(BF)
        if pair == 0:
            dk[: 6 * BLK, :] = dkw
            dv[: 6 * BLK, :] = dvw
        else:
            dk[2 * BLK : 6 * BLK, :] += dkw[: 4 * BLK]
            dv[2 * BLK : 6 * BLK, :] += dvw[: 4 * BLK]
            dk[6 * BLK :, :] = dkw[4 * BLK :]
            dv[6 * BLK :, :] = dvw[4 * BLK :]
    for s, o in enumerate((dq0, dq1, dq2, dq3)):
        o[...] = dqs[lax.rem(z + s, NZ)]
    for j in range(2):
        rim_before[j, 0] = (dk[j * BLK : (j + 1) * BLK, :] * SCALE).astype(BF)
        rim_before[j, 1] = dv[j * BLK : (j + 1) * BLK, :].astype(BF)
        rim_after[j, 0] = (dk[(6 + j) * BLK : (7 + j) * BLK, :] * SCALE).astype(BF)
        rim_after[j, 1] = dv[(6 + j) * BLK : (7 + j) * BLK, :].astype(BF)
    for j in range(4):
        own[j, 0] = dk[(2 + j) * BLK : (3 + j) * BLK, :] * SCALE
        own[j, 1] = dv[(2 + j) * BLK : (3 + j) * BLK, :]


def attend(zh, q, g, recv, before, lo, hi, after, bias, first, heads, group):
    n = heads * HD
    mine = pl.BlockSpec((BLK, HD), lambda h, z: (0, z[0] * group + first + h))
    got = pl.BlockSpec((2, BLK, HD), lambda h, z: (0, 0, h))
    keys = pl.BlockSpec((2, 2, BLK, HD), lambda h, z: (0, 0, 0, first + h))
    flat = pl.BlockSpec((BLK, HD), lambda h, z: (0, h))
    rim = pl.BlockSpec((2, 2, BLK, HD), lambda h, z: (0, 0, 0, h))
    own = pl.BlockSpec((4, 2, BLK, HD), lambda h, z: (0, 0, 0, h))
    shape = jax.ShapeDtypeStruct
    return pl.pallas_call(
        attend_body,
        grid_spec=pltpu.PrefetchScalarGridSpec(
            num_scalar_prefetch=1,
            grid=(heads,),
            in_specs=[mine, mine, got, got, got, keys, keys, keys, keys,
                      pl.BlockSpec((1, 2, 6, 2 * BLK), lambda h, z: (first + h, 0, 0, 0))],
            out_specs=[flat] * 4 + [rim, rim, own],
            scratch_shapes=[
                pltpu.VMEM((4 * BLK, HD), BF),
                pltpu.VMEM((4 * BLK, HD), BF),
                pltpu.VMEM((8 * BLK, HD), BF),
                pltpu.VMEM((8 * BLK, HD), BF),
                pltpu.VMEM((4, BLK, HD), BF),
                pltpu.VMEM((8 * BLK, HD), F32),
                pltpu.VMEM((8 * BLK, HD), F32),
            ],
        ),
        out_shape=[shape((BLK, n), BF)] * 4
        + [shape((2, 2, BLK, n), BF)] * 2
        + [shape((4, 2, BLK, n), F32)],
        cost_estimate=cost(heads * 2 * 5 * 2 * 768 * 256 * 128, 40 * BLK * n * 2),
        compiler_params=grant(24),
    )(zh, q, g, *recv, before, lo, hi, after, bias)


def finish_body(zh, own, from_before, from_after, o0, o1, o2, o3):
    z = zh[0]
    for s, o in enumerate((o0, o1, o2, o3)):
        b = lax.rem(z + s, NZ)

        @pl.when(b < 2)
        def _():
            o[...] = (own[b] + from_before[b].astype(F32)).astype(BF)

        @pl.when(b >= 2)
        def _():
            o[...] = (own[b] + from_after[b - 2].astype(F32)).astype(BF)


def finish(zh, own, from_before, from_after):
    n = own.shape[-1]
    rim = pl.BlockSpec((2, 2, BLK, CW), lambda i, z: (0, 0, 0, i))
    out = pl.BlockSpec((2, BLK, CW), lambda i, z: (0, 0, i))
    return pl.pallas_call(
        finish_body,
        grid_spec=pltpu.PrefetchScalarGridSpec(
            num_scalar_prefetch=1,
            grid=(n // CW,),
            in_specs=[pl.BlockSpec((4, 2, BLK, CW), lambda i, z: (0, 0, 0, i)), rim, rim],
            out_specs=[out] * 4,
        ),
        out_shape=[jax.ShapeDtypeStruct((2, BLK, n), BF)] * 4,
        cost_estimate=cost(0, 32 * BLK * n * 2),
        compiler_params=grant(12),
    )(zh, own, from_before, from_after)


def assemble_body(zh, *refs):
    n_chunks = len(CHUNKS)
    ins, outs = refs[: 8 * n_chunks], refs[8 * n_chunks :]
    t = pl.program_id(0)
    for s in range(NZ):

        @pl.when(t == s)
        def _():
            for c, (first, heads) in enumerate(CHUNKS):
                cols = slice(first * HD, (first + heads) * HD)
                outs[0][:, cols] = ins[8 * c + s][...]
                outs[1][:, cols] = ins[8 * c + 4 + s][0]
                outs[2][:, cols] = ins[8 * c + 4 + s][1]


def assemble(zh, parts, group, width):
    specs, args = [], []
    for dq, dkv in parts:
        for a in (*dq, *dkv):
            specs.append(pl.BlockSpec(a.shape, lambda t, z, nd=a.ndim: (0,) * nd))
            args.append(a)
    out = pl.BlockSpec((BLK, group * HD), lambda t, z: (0, lax.rem(z[0] + NZ - t, NZ)))
    return pl.pallas_call(
        assemble_body,
        grid_spec=pltpu.PrefetchScalarGridSpec(
            num_scalar_prefetch=1, grid=(NZ,), in_specs=specs, out_specs=[out] * 3
        ),
        out_shape=[jax.ShapeDtypeStruct((BLK, width), BF)] * 3,
        cost_estimate=cost(0, 6 * BLK * width * 2),
        compiler_params=grant(24),
        name="assemble",
    )(zh, *args)


def tile_bias(tile_mask, zh, slab, group):
    all_blocks, span = tile_mask.shape[1], tile_mask.shape[2]
    local = lax.dynamic_slice(tile_mask, (zh * group, slab * NZ, 0), (group, NZ, span))
    key_block = slab * NZ + jnp.arange(NZ, dtype=jnp.int32)[:, None] + jnp.arange(span, dtype=jnp.int32)[None] - span // 2
    active = (local != 0) & (key_block >= 0) & (key_block < all_blocks)
    active = active.reshape(group, 2, 2, span)
    left = jnp.pad(active[:, :, 0], ((0, 0), (0, 0), (0, 1)))
    right = jnp.pad(active[:, :, 1], ((0, 0), (0, 0), (1, 0)))
    rows = jnp.stack([left, right], -1)
    return jnp.repeat(jnp.where(rows, 0.0, -jnp.inf).astype(F32), BLK, axis=-1)


def shards(query, key, value, dout, tile_mask):
    n_ctx, n_uly = lax.axis_size("ctx"), lax.axis_size("uly")
    width = query.shape[1]
    group = tile_mask.shape[0] // NZ
    me = lax.axis_index("uly")
    zh_s = lax.rem(me, NZ)
    slab = lax.axis_index("ctx") * (n_uly // NZ) + me // NZ
    zh = zh_s.astype(jnp.int32).reshape(1)
    n_slabs = n_ctx * n_uly // NZ
    rings = [
        [(NZ * i + j, NZ * i + (j + s) % NZ) for i in range(n_uly // NZ) for j in range(NZ)] for s in range(NZ)
    ]
    up = [(NZ * i + j, NZ * (i + 1) + j) for i in range(n_slabs - 1) for j in range(NZ)]
    down = [(b, a) for a, b in up]

    def around(arrays):
        out = []
        for s, a in enumerate(arrays, 1):
            out.append(lax.ppermute(a, "uly", rings[s]))
        return out

    def to_next(a):
        return lax.ppermute(a, ("ctx", "uly"), up)

    def to_prev(a):
        return lax.ppermute(a, ("ctx", "uly"), down)

    bias = tile_bias(tile_mask, zh_s, slab, group)
    kv = around(pack(zh, key, value, 0, group, group))
    qg = []
    behind = kv
    for first, heads in CHUNKS:
        packed = list(pack(zh, query, dout, first, heads, group))
        for s in range(3):
            packed[s], _ = lax.optimization_barrier((packed[s], behind[s]))
        behind = around(packed)
        qg.append(behind)
    lo, hi = unpack(zh, key, value, kv, group)
    before, after = to_next(hi), to_prev(lo)
    parts = []
    for (first, heads), recv in zip(CHUNKS, qg):
        *dq, rim_before, rim_after, own = attend(
            zh, query, dout, recv, before, lo, hi, after, bias, first, heads, group
        )
        from_after, from_before = to_prev(rim_before), to_next(rim_after)
        back_q = [dq[0], *around(dq[1:])]
        dkv = finish(zh, own, from_before, from_after)
        back_kv = [dkv[0], *around(dkv[1:])]
        parts.append((back_q, back_kv))
    return assemble(zh, parts, group, width)


def solution(mesh):
    rows = P(("ctx", "uly"), None)
    return jax.shard_map(
        shards,
        mesh=mesh,
        in_specs=(rows, rows, rows, rows, P()),
        out_specs=(rows, rows, rows),
        check_vma=False,
    )
```

```python
import math

import jax
import jax.numpy as jnp
from jax import lax
from jax.experimental import pallas as pl
from jax.experimental.pallas import tpu as pltpu
from jax.sharding import PartitionSpec as P


BLK = 128
HD = 128
NZ = 4
CHUNKS = ((0, 6), (6, 4))
CW = 256
SCALE = 1.0 / math.sqrt(HD)
EXP2_SCALE = SCALE / math.log(2.0)
BF = jnp.bfloat16
F32 = jnp.float32


MIB = 1 << 20


def grant(mib):
    return pltpu.CompilerParams(vmem_limit_bytes=mib * MIB)


def cost(flops, nbytes):
    return pl.CostEstimate(flops=flops, bytes_accessed=nbytes, transcendentals=0)


def pack_body(zh, a1, a2, a3, b1, b2, b3, o1, o2, o3):
    for a, b, o in ((a1, b1, o1), (a2, b2, o2), (a3, b3, o3)):
        o[0] = a[...]
        o[1] = b[...]


def pack(zh, a, b, first, heads, group):
    per, off, steps = group * HD // CW, first * HD // CW, heads * HD // CW

    def src(s):
        return pl.BlockSpec((BLK, CW), lambda i, z: (0, lax.rem(z[0] + s, NZ) * per + off + i))

    out = pl.BlockSpec((2, BLK, CW), lambda i, z: (0, 0, i))
    n = heads * HD
    return pl.pallas_call(
        pack_body,
        grid_spec=pltpu.PrefetchScalarGridSpec(
            num_scalar_prefetch=1,
            grid=(steps,),
            in_specs=[src(1), src(2), src(3), src(1), src(2), src(3)],
            out_specs=[out, out, out],
        ),
        out_shape=[jax.ShapeDtypeStruct((2, BLK, n), BF)] * 3,
        cost_estimate=cost(0, 12 * BLK * n * 2),
        compiler_params=grant(8),
    )(zh, a, a, a, b, b, b)


def unpack_body(zh, k, v, r1, r2, r3, lo, hi):
    z = zh[0]
    for s, (kk, vv) in enumerate(((k, v), (r1.at[0], r1.at[1]), (r2.at[0], r2.at[1]), (r3.at[0], r3.at[1]))):
        b = lax.rem(z + NZ - s, NZ)

        @pl.when(b < 2)
        def _():
            lo[b, 0] = kk[...]
            lo[b, 1] = vv[...]

        @pl.when(b >= 2)
        def _():
            hi[b - 2, 0] = kk[...]
            hi[b - 2, 1] = vv[...]


def unpack(zh, k, v, recv, group):
    n = group * HD
    per = n // CW
    own = pl.BlockSpec((BLK, CW), lambda i, z: (0, z[0] * per + i))
    got = pl.BlockSpec((2, BLK, CW), lambda i, z: (0, 0, i))
    half = pl.BlockSpec((2, 2, BLK, CW), lambda i, z: (0, 0, 0, i))
    return pl.pallas_call(
        unpack_body,
        grid_spec=pltpu.PrefetchScalarGridSpec(
            num_scalar_prefetch=1, grid=(per,), in_specs=[own, own, got, got, got], out_specs=[half, half]
        ),
        out_shape=[jax.ShapeDtypeStruct((2, 2, BLK, n), BF)] * 2,
        cost_estimate=cost(0, 16 * BLK * n * 2),
        compiler_params=grant(10),
        name="unpack",
    )(zh, k, v, *recv)


def attend_body(zh, q0, g0, x1, x2, x3, before, lo, hi, after, bias,
                dq0, dq1, dq2, dq3, rim_before, rim_after, own,
                qs, gs, ks, vs, dqs, dk, dv):
    z = zh[0]
    for s, (qq, gg) in enumerate(((q0, g0), (x1.at[0], x1.at[1]), (x2.at[0], x2.at[1]), (x3.at[0], x3.at[1]))):
        row = pl.multiple_of(lax.rem(z + NZ - s, NZ) * BLK, BLK)
        qs[pl.ds(row, BLK), :] = qq[...]
        gs[pl.ds(row, BLK), :] = gg[...]
    for i, (ref, j) in enumerate(
        ((before, 0), (before, 1), (lo, 0), (lo, 1), (hi, 0), (hi, 1), (after, 0), (after, 1))
    ):
        ks[i * BLK : (i + 1) * BLK, :] = ref[j, 0]
        vs[i * BLK : (i + 1) * BLK, :] = ref[j, 1]
    nt = (((1,), (1,)), ((), ()))
    tn = (((0,), (0,)), ((), ()))
    nn = (((1,), (0,)), ((), ()))
    for pair in range(2):
        r0 = pair * 2 * BLK
        kw, vw = ks[r0 : r0 + 6 * BLK, :], vs[r0 : r0 + 6 * BLK, :]
        q, g = qs[r0 : r0 + 2 * BLK, :], gs[r0 : r0 + 2 * BLK, :]
        st = lax.dot_general(kw, q, nt, preferred_element_type=F32)
        st = st.reshape(6, BLK, 2 * BLK) + bias[0, pair][:, None, :]
        top = jnp.max(jnp.max(st, axis=0), axis=0, keepdims=True)[None]
        e = jnp.exp2((st - top) * EXP2_SCALE)
        total = jnp.sum(jnp.sum(e, axis=0), axis=0, keepdims=True)[None]
        p = e * (1.0 / total)
        dp = lax.dot_general(vw, g, nt, preferred_element_type=F32).reshape(6, BLK, 2 * BLK)
        delta = jnp.sum(jnp.sum(p * dp, axis=0), axis=0, keepdims=True)[None]
        ds = (p * (dp - delta)).astype(BF).reshape(6 * BLK, 2 * BLK)
        pb = p.astype(BF).reshape(6 * BLK, 2 * BLK)
        dvw = lax.dot_general(pb, g, nn, preferred_element_type=F32)
        dkw = lax.dot_general(ds, q, nn, preferred_element_type=F32)
        dqw = lax.dot_general(ds, kw, tn, preferred_element_type=F32) * SCALE
        dqs[2 * pair] = dqw[:BLK].astype(BF)
        dqs[2 * pair + 1] = dqw[BLK:].astype(BF)
        if pair == 0:
            dk[: 6 * BLK, :] = dkw
            dv[: 6 * BLK, :] = dvw
        else:
            dk[2 * BLK : 6 * BLK, :] += dkw[: 4 * BLK]
            dv[2 * BLK : 6 * BLK, :] += dvw[: 4 * BLK]
            dk[6 * BLK :, :] = dkw[4 * BLK :]
            dv[6 * BLK :, :] = dvw[4 * BLK :]
    for s, o in enumerate((dq0, dq1, dq2, dq3)):
        o[...] = dqs[lax.rem(z + s, NZ)]
    for j in range(2):
        rim_before[j, 0] = (dk[j * BLK : (j + 1) * BLK, :] * SCALE).astype(BF)
        rim_before[j, 1] = dv[j * BLK : (j + 1) * BLK, :].astype(BF)
        rim_after[j, 0] = (dk[(6 + j) * BLK : (7 + j) * BLK, :] * SCALE).astype(BF)
        rim_after[j, 1] = dv[(6 + j) * BLK : (7 + j) * BLK, :].astype(BF)
    for j in range(4):
        own[j, 0] = dk[(2 + j) * BLK : (3 + j) * BLK, :] * SCALE
        own[j, 1] = dv[(2 + j) * BLK : (3 + j) * BLK, :]


def attend(zh, q, g, recv, before, lo, hi, after, bias, first, heads, group):
    n = heads * HD
    mine = pl.BlockSpec((BLK, HD), lambda h, z: (0, z[0] * group + first + h))
    got = pl.BlockSpec((2, BLK, HD), lambda h, z: (0, 0, h))
    keys = pl.BlockSpec((2, 2, BLK, HD), lambda h, z: (0, 0, 0, first + h))
    flat = pl.BlockSpec((BLK, HD), lambda h, z: (0, h))
    rim = pl.BlockSpec((2, 2, BLK, HD), lambda h, z: (0, 0, 0, h))
    own = pl.BlockSpec((4, 2, BLK, HD), lambda h, z: (0, 0, 0, h))
    shape = jax.ShapeDtypeStruct
    return pl.pallas_call(
        attend_body,
        grid_spec=pltpu.PrefetchScalarGridSpec(
            num_scalar_prefetch=1,
            grid=(heads,),
            in_specs=[mine, mine, got, got, got, keys, keys, keys, keys,
                      pl.BlockSpec((1, 2, 6, 2 * BLK), lambda h, z: (first + h, 0, 0, 0))],
            out_specs=[flat] * 4 + [rim, rim, own],
            scratch_shapes=[
                pltpu.VMEM((4 * BLK, HD), BF),
                pltpu.VMEM((4 * BLK, HD), BF),
                pltpu.VMEM((8 * BLK, HD), BF),
                pltpu.VMEM((8 * BLK, HD), BF),
                pltpu.VMEM((4, BLK, HD), BF),
                pltpu.VMEM((8 * BLK, HD), F32),
                pltpu.VMEM((8 * BLK, HD), F32),
            ],
        ),
        out_shape=[shape((BLK, n), BF)] * 4
        + [shape((2, 2, BLK, n), BF)] * 2
        + [shape((4, 2, BLK, n), F32)],
        cost_estimate=cost(heads * 2 * 5 * 2 * 768 * 256 * 128, 40 * BLK * n * 2),
        compiler_params=grant(24),
    )(zh, q, g, *recv, before, lo, hi, after, bias)


def finish_body(zh, own, from_before, from_after, o0, o1, o2, o3):
    z = zh[0]
    for s, o in enumerate((o0, o1, o2, o3)):
        b = lax.rem(z + s, NZ)

        @pl.when(b < 2)
        def _():
            o[...] = (own[b] + from_before[b].astype(F32)).astype(BF)

        @pl.when(b >= 2)
        def _():
            o[...] = (own[b] + from_after[b - 2].astype(F32)).astype(BF)


def finish(zh, own, from_before, from_after):
    n = own.shape[-1]
    rim = pl.BlockSpec((2, 2, BLK, CW), lambda i, z: (0, 0, 0, i))
    out = pl.BlockSpec((2, BLK, CW), lambda i, z: (0, 0, i))
    return pl.pallas_call(
        finish_body,
        grid_spec=pltpu.PrefetchScalarGridSpec(
            num_scalar_prefetch=1,
            grid=(n // CW,),
            in_specs=[pl.BlockSpec((4, 2, BLK, CW), lambda i, z: (0, 0, 0, i)), rim, rim],
            out_specs=[out] * 4,
        ),
        out_shape=[jax.ShapeDtypeStruct((2, BLK, n), BF)] * 4,
        cost_estimate=cost(0, 32 * BLK * n * 2),
        compiler_params=grant(12),
    )(zh, own, from_before, from_after)


def assemble_body(zh, *refs):
    n_chunks = len(CHUNKS)
    ins, outs = refs[: 8 * n_chunks], refs[8 * n_chunks :]
    t = pl.program_id(0)
    for s in range(NZ):

        @pl.when(t == s)
        def _():
            for c, (first, heads) in enumerate(CHUNKS):
                cols = slice(first * HD, (first + heads) * HD)
                outs[0][:, cols] = ins[8 * c + s][...]
                outs[1][:, cols] = ins[8 * c + 4 + s][0]
                outs[2][:, cols] = ins[8 * c + 4 + s][1]


def assemble(zh, parts, group, width):
    specs, args = [], []
    for dq, dkv in parts:
        for a in (*dq, *dkv):
            specs.append(pl.BlockSpec(a.shape, lambda t, z, nd=a.ndim: (0,) * nd))
            args.append(a)
    out = pl.BlockSpec((BLK, group * HD), lambda t, z: (0, lax.rem(z[0] + NZ - t, NZ)))
    return pl.pallas_call(
        assemble_body,
        grid_spec=pltpu.PrefetchScalarGridSpec(
            num_scalar_prefetch=1, grid=(NZ,), in_specs=specs, out_specs=[out] * 3
        ),
        out_shape=[jax.ShapeDtypeStruct((BLK, width), BF)] * 3,
        cost_estimate=cost(0, 6 * BLK * width * 2),
        compiler_params=grant(24),
        name="assemble",
    )(zh, *args)


def tile_bias(tile_mask, zh, slab, group):
    all_blocks, span = tile_mask.shape[1], tile_mask.shape[2]
    local = lax.dynamic_slice(tile_mask, (zh * group, slab * NZ, 0), (group, NZ, span))
    key_block = slab * NZ + jnp.arange(NZ, dtype=jnp.int32)[:, None] + jnp.arange(span, dtype=jnp.int32)[None] - span // 2
    active = (local != 0) & (key_block >= 0) & (key_block < all_blocks)
    active = active.reshape(group, 2, 2, span)
    left = jnp.pad(active[:, :, 0], ((0, 0), (0, 0), (0, 1)))
    right = jnp.pad(active[:, :, 1], ((0, 0), (0, 0), (1, 0)))
    rows = jnp.stack([left, right], -1)
    return jnp.repeat(jnp.where(rows, 0.0, -jnp.inf).astype(F32), BLK, axis=-1)


def shards(query, key, value, dout, tile_mask):
    n_ctx, n_uly = lax.axis_size("ctx"), lax.axis_size("uly")
    width = query.shape[1]
    group = tile_mask.shape[0] // NZ
    me = lax.axis_index("uly")
    zh_s = lax.rem(me, NZ)
    slab = lax.axis_index("ctx") * (n_uly // NZ) + me // NZ
    zh = zh_s.astype(jnp.int32).reshape(1)
    n_slabs = n_ctx * n_uly // NZ
    rings = [
        [(NZ * i + j, NZ * i + (j + s) % NZ) for i in range(n_uly // NZ) for j in range(NZ)] for s in range(NZ)
    ]
    up = [(NZ * i + j, NZ * (i + 1) + j) for i in range(n_slabs - 1) for j in range(NZ)]
    down = [(b, a) for a, b in up]

    def around(arrays):
        out = []
        for s, a in enumerate(arrays, 1):
            out.append(lax.ppermute(a, "uly", rings[s]))
        return out

    def to_next(a):
        return lax.ppermute(a, ("ctx", "uly"), up)

    def to_prev(a):
        return lax.ppermute(a, ("ctx", "uly"), down)

    bias = tile_bias(tile_mask, zh_s, slab, group)
    kv = around(pack(zh, key, value, 0, group, group))
    qg = [around(pack(zh, query, dout, first, heads, group)) for first, heads in CHUNKS]
    lo, hi = unpack(zh, key, value, kv, group)
    before, after = to_next(hi), to_prev(lo)
    parts = []
    for (first, heads), recv in zip(CHUNKS, qg):
        *dq, rim_before, rim_after, own = attend(
            zh, query, dout, recv, before, lo, hi, after, bias, first, heads, group
        )
        from_after, from_before = to_prev(rim_before), to_next(rim_after)
        back_q = [dq[0], *around(dq[1:])]
        dkv = finish(zh, own, from_before, from_after)
        back_kv = [dkv[0], *around(dkv[1:])]
        parts.append((back_q, back_kv))
    return assemble(zh, parts, group, width)


def solution(mesh):
    rows = P(("ctx", "uly"), None)
    return jax.shard_map(
        shards,
        mesh=mesh,
        in_specs=(rows, rows, rows, rows, P()),
        out_specs=(rows, rows, rows),
        check_vma=False,
    )
```

```python
import math

import jax
import jax.numpy as jnp
from jax import lax
from jax.experimental import pallas as pl
from jax.experimental.pallas import tpu as pltpu
from jax.sharding import PartitionSpec as P


BLK = 128
HD = 128
NZ = 4
CHUNKS = ((0, 6), (6, 4))
CW = 256
SCALE = 1.0 / math.sqrt(HD)
EXP2_SCALE = SCALE / math.log(2.0)
BF = jnp.bfloat16
F32 = jnp.float32


MIB = 1 << 20


def grant(mib):
    return pltpu.CompilerParams(vmem_limit_bytes=mib * MIB)


def cost(flops, nbytes):
    return pl.CostEstimate(flops=flops, bytes_accessed=nbytes, transcendentals=0)


def pack_body(zh, *refs):
    ins, (plus, minus) = refs[:-2], refs[-2:]
    m = len(ins) // 2
    for i in range(m):
        plus[i] = ins[i][...]
        minus[i] = ins[m + i][...]


def pack(zh, plus, minus, first, heads, group):
    per, off, steps = group * HD // CW, first * HD // CW, heads * HD // CW
    n, m = heads * HD, len(plus)

    def src(s):
        return pl.BlockSpec((BLK, CW), lambda i, z: (0, lax.rem(z[0] + s, NZ) * per + off + i))

    out = pl.BlockSpec((m, BLK, CW), lambda i, z: (0, 0, i))
    return pl.pallas_call(
        pack_body,
        grid_spec=pltpu.PrefetchScalarGridSpec(
            num_scalar_prefetch=1,
            grid=(steps,),
            in_specs=[src(s) for _, s in (*plus, *minus)],
            out_specs=[out, out],
        ),
        out_shape=[jax.ShapeDtypeStruct((m, BLK, n), BF)] * 2,
        cost_estimate=cost(0, 4 * m * BLK * n * 2),
        compiler_params=grant(56),
    )(zh, *[a for a, _ in (*plus, *minus)])


def unpack_body(zh, k, v, mp, mm, fp, fm, lo, hi):
    z = zh[0]
    for s, (kk, vv) in enumerate(((k, v), (mp.at[0], mp.at[1]), (fp.at[0], fm.at[0]), (mm.at[0], mm.at[1]))):
        b = lax.rem(z + NZ - s, NZ)

        @pl.when(b < 2)
        def _():
            lo[b, 0] = kk[...]
            lo[b, 1] = vv[...]

        @pl.when(b >= 2)
        def _():
            hi[b - 2, 0] = kk[...]
            hi[b - 2, 1] = vv[...]


def unpack(zh, k, v, recv, first, heads, group):
    n = heads * HD
    per, off = group * HD // CW, first * HD // CW
    own = pl.BlockSpec((BLK, CW), lambda i, z: (0, z[0] * per + off + i))
    two = pl.BlockSpec((2, BLK, CW), lambda i, z: (0, 0, i))
    one = pl.BlockSpec((1, BLK, CW), lambda i, z: (0, 0, i))
    half = pl.BlockSpec((2, 2, BLK, CW), lambda i, z: (0, 0, 0, i))
    return pl.pallas_call(
        unpack_body,
        grid_spec=pltpu.PrefetchScalarGridSpec(
            num_scalar_prefetch=1, grid=(n // CW,), in_specs=[own, own, two, two, one, one], out_specs=[half, half]
        ),
        out_shape=[jax.ShapeDtypeStruct((2, 2, BLK, n), BF)] * 2,
        cost_estimate=cost(0, 16 * BLK * n * 2),
        compiler_params=grant(8),
    )(zh, k, v, *recv)


def attend_body(zh, q0, g0, mp, mm, fp, fm, before, lo, hi, after, bias,
                dq0, dq1, dq2, dq3, rim_before, rim_after, own,
                qs, gs, ks, vs, dqs, dk, dv):
    z = zh[0]
    for s, (qq, gg) in enumerate(((q0, g0), (mp.at[0], mp.at[1]), (fp.at[0], fm.at[0]), (mm.at[0], mm.at[1]))):
        row = pl.multiple_of(lax.rem(z + NZ - s, NZ) * BLK, BLK)
        qs[pl.ds(row, BLK), :] = qq[...]
        gs[pl.ds(row, BLK), :] = gg[...]
    for i, (ref, j) in enumerate(
        ((before, 0), (before, 1), (lo, 0), (lo, 1), (hi, 0), (hi, 1), (after, 0), (after, 1))
    ):
        ks[i * BLK : (i + 1) * BLK, :] = ref[j, 0]
        vs[i * BLK : (i + 1) * BLK, :] = ref[j, 1]
    nt = (((1,), (1,)), ((), ()))
    tn = (((0,), (0,)), ((), ()))
    nn = (((1,), (0,)), ((), ()))
    for pair in range(2):
        r0 = pair * 2 * BLK
        kw, vw = ks[r0 : r0 + 6 * BLK, :], vs[r0 : r0 + 6 * BLK, :]
        q, g = qs[r0 : r0 + 2 * BLK, :], gs[r0 : r0 + 2 * BLK, :]
        st = lax.dot_general(kw, q, nt, preferred_element_type=F32)
        st = st.reshape(6, BLK, 2 * BLK) + bias[0, pair][:, None, :]
        top = jnp.max(jnp.max(st, axis=0), axis=0, keepdims=True)[None]
        e = jnp.exp2((st - top) * EXP2_SCALE)
        total = jnp.sum(jnp.sum(e, axis=0), axis=0, keepdims=True)[None]
        p = e * (1.0 / total)
        dp = lax.dot_general(vw, g, nt, preferred_element_type=F32).reshape(6, BLK, 2 * BLK)
        delta = jnp.sum(jnp.sum(p * dp, axis=0), axis=0, keepdims=True)[None]
        ds = (p * (dp - delta)).astype(BF).reshape(6 * BLK, 2 * BLK)
        pb = p.astype(BF).reshape(6 * BLK, 2 * BLK)
        dvw = lax.dot_general(pb, g, nn, preferred_element_type=F32)
        dkw = lax.dot_general(ds, q, nn, preferred_element_type=F32)
        dqw = lax.dot_general(ds, kw, tn, preferred_element_type=F32) * SCALE
        dqs[2 * pair] = dqw[:BLK].astype(BF)
        dqs[2 * pair + 1] = dqw[BLK:].astype(BF)
        if pair == 0:
            dk[: 6 * BLK, :] = dkw
            dv[: 6 * BLK, :] = dvw
        else:
            dk[2 * BLK : 6 * BLK, :] += dkw[: 4 * BLK]
            dv[2 * BLK : 6 * BLK, :] += dvw[: 4 * BLK]
            dk[6 * BLK :, :] = dkw[4 * BLK :]
            dv[6 * BLK :, :] = dvw[4 * BLK :]
    for s, o in enumerate((dq0, dq1, dq2, dq3)):
        o[...] = dqs[lax.rem(z + s, NZ)]
    for j in range(2):
        rim_before[j, 0] = (dk[j * BLK : (j + 1) * BLK, :] * SCALE).astype(BF)
        rim_before[j, 1] = dv[j * BLK : (j + 1) * BLK, :].astype(BF)
        rim_after[j, 0] = (dk[(6 + j) * BLK : (7 + j) * BLK, :] * SCALE).astype(BF)
        rim_after[j, 1] = dv[(6 + j) * BLK : (7 + j) * BLK, :].astype(BF)
    for j in range(4):
        own[j, 0] = dk[(2 + j) * BLK : (3 + j) * BLK, :] * SCALE
        own[j, 1] = dv[(2 + j) * BLK : (3 + j) * BLK, :]


def attend(zh, q, g, recv, before, lo, hi, after, bias, first, heads, group):
    n = heads * HD
    mine = pl.BlockSpec((BLK, HD), lambda h, z: (0, z[0] * group + first + h))
    two = pl.BlockSpec((2, BLK, HD), lambda h, z: (1, 0, h))
    one = pl.BlockSpec((1, BLK, HD), lambda h, z: (1, 0, h))
    flat = pl.BlockSpec((BLK, HD), lambda h, z: (0, h))
    rim = pl.BlockSpec((2, 2, BLK, HD), lambda h, z: (0, 0, 0, h))
    own = pl.BlockSpec((4, 2, BLK, HD), lambda h, z: (0, 0, 0, h))
    shape = jax.ShapeDtypeStruct
    return pl.pallas_call(
        attend_body,
        grid_spec=pltpu.PrefetchScalarGridSpec(
            num_scalar_prefetch=1,
            grid=(heads,),
            in_specs=[mine, mine, two, two, one, one, rim, rim, rim, rim,
                      pl.BlockSpec((1, 2, 6, 2 * BLK), lambda h, z: (first + h, 0, 0, 0))],
            out_specs=[flat] * 4 + [rim, rim, own],
            scratch_shapes=[
                pltpu.VMEM((4 * BLK, HD), BF),
                pltpu.VMEM((4 * BLK, HD), BF),
                pltpu.VMEM((8 * BLK, HD), BF),
                pltpu.VMEM((8 * BLK, HD), BF),
                pltpu.VMEM((4, BLK, HD), BF),
                pltpu.VMEM((8 * BLK, HD), F32),
                pltpu.VMEM((8 * BLK, HD), F32),
            ],
        ),
        out_shape=[shape((BLK, n), BF)] * 4
        + [shape((2, 2, BLK, n), BF)] * 2
        + [shape((4, 2, BLK, n), F32)],
        cost_estimate=cost(heads * 2 * 5 * 2 * 768 * 256 * 128, 40 * BLK * n * 2),
        compiler_params=grant(24),
    )(zh, q, g, *recv, before, lo, hi, after, bias)


def finish_body(zh, own, from_before, from_after, o0, o1, o2, o3):
    z = zh[0]
    for s, o in enumerate((o0, o1, o2, o3)):
        b = lax.rem(z + s, NZ)

        @pl.when(b < 2)
        def _():
            o[...] = (own[b] + from_before[b].astype(F32)).astype(BF)

        @pl.when(b >= 2)
        def _():
            o[...] = (own[b] + from_after[b - 2].astype(F32)).astype(BF)


def finish(zh, own, from_before, from_after):
    n = own.shape[-1]
    rim = pl.BlockSpec((2, 2, BLK, CW), lambda i, z: (0, 0, 0, i))
    out = pl.BlockSpec((2, BLK, CW), lambda i, z: (0, 0, i))
    return pl.pallas_call(
        finish_body,
        grid_spec=pltpu.PrefetchScalarGridSpec(
            num_scalar_prefetch=1,
            grid=(n // CW,),
            in_specs=[pl.BlockSpec((4, 2, BLK, CW), lambda i, z: (0, 0, 0, i)), rim, rim],
            out_specs=[out] * 4,
        ),
        out_shape=[jax.ShapeDtypeStruct((2, BLK, n), BF)] * 4,
        cost_estimate=cost(0, 32 * BLK * n * 2),
        compiler_params=grant(12),
    )(zh, own, from_before, from_after)


def assemble_body(zh, *refs):
    n_chunks = len(CHUNKS)
    ins, outs = refs[: 8 * n_chunks], refs[8 * n_chunks :]
    t = pl.program_id(0)
    for s in range(NZ):

        @pl.when(t == s)
        def _():
            for c, (first, heads) in enumerate(CHUNKS):
                cols = slice(first * HD, (first + heads) * HD)
                outs[0][:, cols] = ins[8 * c + s][...]
                outs[1][:, cols] = ins[8 * c + 4 + s][0]
                outs[2][:, cols] = ins[8 * c + 4 + s][1]


def assemble(zh, parts, group, width):
    specs, args = [], []
    for dq, dkv in parts:
        for a in (*dq, *dkv):
            specs.append(pl.BlockSpec(a.shape, lambda t, z, nd=a.ndim: (0,) * nd))
            args.append(a)
    out = pl.BlockSpec((BLK, group * HD), lambda t, z: (0, lax.rem(z[0] + NZ - t, NZ)))
    return pl.pallas_call(
        assemble_body,
        grid_spec=pltpu.PrefetchScalarGridSpec(
            num_scalar_prefetch=1, grid=(NZ,), in_specs=specs, out_specs=[out] * 3
        ),
        out_shape=[jax.ShapeDtypeStruct((BLK, width), BF)] * 3,
        cost_estimate=cost(0, 6 * BLK * width * 2),
        compiler_params=grant(24),
        name="assemble",
    )(zh, *args)


def tile_bias(tile_mask, zh, slab, group):
    all_blocks, span = tile_mask.shape[1], tile_mask.shape[2]
    local = lax.dynamic_slice(tile_mask, (zh * group, slab * NZ, 0), (group, NZ, span))
    key_block = slab * NZ + jnp.arange(NZ, dtype=jnp.int32)[:, None] + jnp.arange(span, dtype=jnp.int32)[None] - span // 2
    active = (local != 0) & (key_block >= 0) & (key_block < all_blocks)
    active = active.reshape(group, 2, 2, span)
    left = jnp.pad(active[:, :, 0], ((0, 0), (0, 0), (0, 1)))
    right = jnp.pad(active[:, :, 1], ((0, 0), (0, 0), (1, 0)))
    rows = jnp.stack([left, right], -1)
    return jnp.repeat(jnp.where(rows, 0.0, -jnp.inf).astype(F32), BLK, axis=-1)


def shards(query, key, value, dout, tile_mask):
    n_ctx, n_uly = lax.axis_size("ctx"), lax.axis_size("uly")
    width = query.shape[1]
    group = tile_mask.shape[0] // NZ
    me = lax.axis_index("uly")
    zh_s = lax.rem(me, NZ)
    slab = lax.axis_index("ctx") * (n_uly // NZ) + me // NZ
    zh = zh_s.astype(jnp.int32).reshape(1)
    n_slabs = n_ctx * n_uly // NZ
    rings = [
        [(NZ * i + j, NZ * i + (j + s) % NZ) for i in range(n_uly // NZ) for j in range(NZ)] for s in range(NZ)
    ]
    up = [(NZ * i + j, NZ * (i + 1) + j) for i in range(n_slabs - 1) for j in range(NZ)]
    down = [(b, a) for a, b in up]

    def move(axes, perm, a):
        return lax.ppermute(a, axes, perm)

    def around(arrays):
        return [move("uly", rings[s], a) for s, a in enumerate(arrays, 1)]

    def to_next(a):
        return move(("ctx", "uly"), up, a)

    def to_prev(a):
        return move(("ctx", "uly"), down, a)

    bias = tile_bias(tile_mask, zh_s, slab, group)
    parts = []
    for first, heads in CHUNKS:
        rp, rm = pack(zh, ((key, 2), (query, 2)), ((value, 2), (dout, 2)), first, heads, group)
        mp, mm = pack(
            zh, tuple((a, 1) for a in (key, value, query, dout)),
            tuple((a, 3) for a in (key, value, query, dout)), first, heads, group,
        )
        rp, rm = move("uly", rings[1], rp), move("uly", rings[3], rm)
        mp, mm = move("uly", rings[1], mp), move("uly", rings[3], mm)
        fp, fm = move("uly", rings[1], rp), move("uly", rings[3], rm)
        recv = (mp, mm, fp, fm)
        lo, hi = unpack(zh, key, value, recv, first, heads, group)
        before, after = to_next(hi), to_prev(lo)
        *dq, rim_before, rim_after, own = attend(
            zh, query, dout, recv, before, lo, hi, after, bias, first, heads, group
        )
        from_after, from_before = to_prev(rim_before), to_next(rim_after)
        back_q = [dq[0], *around(dq[1:])]
        dkv = finish(zh, own, from_before, from_after)
        back_kv = [dkv[0], *around(dkv[1:])]
        parts.append((back_q, back_kv))
    return assemble(zh, parts, group, width)


def solution(mesh):
    rows = P(("ctx", "uly"), None)
    return jax.shard_map(
        shards,
        mesh=mesh,
        in_specs=(rows, rows, rows, rows, P()),
        out_specs=(rows, rows, rows),
        check_vma=False,
    )
```

```python
import math

import jax
import jax.numpy as jnp
from jax import lax
from jax.experimental import pallas as pl
from jax.experimental.pallas import tpu as pltpu
from jax.sharding import PartitionSpec as P


BLK = 128
HD = 128
NZ = 4
CHUNKS = ((0, 6), (6, 4))
CW = 256
SCALE = 1.0 / math.sqrt(HD)
EXP2_SCALE = SCALE / math.log(2.0)
BF = jnp.bfloat16
F32 = jnp.float32


MIB = 1 << 20


def grant(mib):
    return pltpu.CompilerParams(vmem_limit_bytes=mib * MIB)


def cost(flops, nbytes):
    return pl.CostEstimate(flops=flops, bytes_accessed=nbytes, transcendentals=0)


def pack_body(zh, *refs):
    ins, (plus, minus) = refs[:-2], refs[-2:]
    m = len(ins) // 2
    for i in range(m):
        plus[i] = ins[i][...]
        minus[i] = ins[m + i][...]


def pack(zh, plus, minus, first, heads, group, wide=CW):
    per, off, steps = group * HD // wide, first * HD // wide, heads * HD // wide
    n, m = heads * HD, len(plus)

    def src(s):
        return pl.BlockSpec((BLK, wide), lambda i, z: (0, lax.rem(z[0] + s, NZ) * per + off + i))

    out = pl.BlockSpec((m, BLK, wide), lambda i, z: (0, 0, i))
    return pl.pallas_call(
        pack_body,
        grid_spec=pltpu.PrefetchScalarGridSpec(
            num_scalar_prefetch=1,
            grid=(steps,),
            in_specs=[src(s) for _, s in (*plus, *minus)],
            out_specs=[out, out],
        ),
        out_shape=[jax.ShapeDtypeStruct((m, BLK, n), BF)] * 2,
        cost_estimate=cost(0, 4 * m * BLK * n * 2),
        compiler_params=grant(56),
    )(zh, *[a for a, _ in (*plus, *minus)])


def unpack_body(zh, k, v, mp, mm, fp, fm, lo, hi):
    z = zh[0]
    for s, (kk, vv) in enumerate(((k, v), (mp.at[0], mp.at[1]), (fp.at[0], fm.at[0]), (mm.at[0], mm.at[1]))):
        b = lax.rem(z + NZ - s, NZ)

        @pl.when(b < 2)
        def _():
            lo[b, 0] = kk[...]
            lo[b, 1] = vv[...]

        @pl.when(b >= 2)
        def _():
            hi[b - 2, 0] = kk[...]
            hi[b - 2, 1] = vv[...]


def unpack(zh, k, v, recv, first, heads, group):
    n = heads * HD
    per, off = group * HD // CW, first * HD // CW
    own = pl.BlockSpec((BLK, CW), lambda i, z: (0, z[0] * per + off + i))
    two = pl.BlockSpec((2, BLK, CW), lambda i, z: (0, 0, off + i))
    one = pl.BlockSpec((1, BLK, CW), lambda i, z: (0, 0, off + i))
    half = pl.BlockSpec((2, 2, BLK, CW), lambda i, z: (0, 0, 0, i))
    return pl.pallas_call(
        unpack_body,
        grid_spec=pltpu.PrefetchScalarGridSpec(
            num_scalar_prefetch=1, grid=(n // CW,), in_specs=[own, own, two, two, one, one], out_specs=[half, half]
        ),
        out_shape=[jax.ShapeDtypeStruct((2, 2, BLK, n), BF)] * 2,
        cost_estimate=cost(0, 16 * BLK * n * 2),
        compiler_params=grant(8),
    )(zh, k, v, *recv)


def attend_body(zh, q0, g0, mp, mm, fp, fm, before, lo, hi, after, bias,
                dq0, dq1, dq2, dq3, rim_before, rim_after, own,
                qs, gs, ks, vs, dqs, dk, dv):
    z = zh[0]
    for s, (qq, gg) in enumerate(((q0, g0), (mp.at[0], mp.at[1]), (fp.at[0], fm.at[0]), (mm.at[0], mm.at[1]))):
        row = pl.multiple_of(lax.rem(z + NZ - s, NZ) * BLK, BLK)
        qs[pl.ds(row, BLK), :] = qq[...]
        gs[pl.ds(row, BLK), :] = gg[...]
    for i, (ref, j) in enumerate(
        ((before, 0), (before, 1), (lo, 0), (lo, 1), (hi, 0), (hi, 1), (after, 0), (after, 1))
    ):
        ks[i * BLK : (i + 1) * BLK, :] = ref[j, 0]
        vs[i * BLK : (i + 1) * BLK, :] = ref[j, 1]
    nt = (((1,), (1,)), ((), ()))
    tn = (((0,), (0,)), ((), ()))
    nn = (((1,), (0,)), ((), ()))
    for pair in range(2):
        r0 = pair * 2 * BLK
        kw, vw = ks[r0 : r0 + 6 * BLK, :], vs[r0 : r0 + 6 * BLK, :]
        q, g = qs[r0 : r0 + 2 * BLK, :], gs[r0 : r0 + 2 * BLK, :]
        st = lax.dot_general(kw, q, nt, preferred_element_type=F32)
        st = st.reshape(6, BLK, 2 * BLK) + bias[0, pair][:, None, :]
        top = jnp.max(jnp.max(st, axis=0), axis=0, keepdims=True)[None]
        e = jnp.exp2((st - top) * EXP2_SCALE)
        total = jnp.sum(jnp.sum(e, axis=0), axis=0, keepdims=True)[None]
        p = e * (1.0 / total)
        dp = lax.dot_general(vw, g, nt, preferred_element_type=F32).reshape(6, BLK, 2 * BLK)
        delta = jnp.sum(jnp.sum(p * dp, axis=0), axis=0, keepdims=True)[None]
        ds = (p * (dp - delta)).astype(BF).reshape(6 * BLK, 2 * BLK)
        pb = p.astype(BF).reshape(6 * BLK, 2 * BLK)
        dvw = lax.dot_general(pb, g, nn, preferred_element_type=F32)
        dkw = lax.dot_general(ds, q, nn, preferred_element_type=F32)
        dqw = lax.dot_general(ds, kw, tn, preferred_element_type=F32) * SCALE
        dqs[2 * pair] = dqw[:BLK].astype(BF)
        dqs[2 * pair + 1] = dqw[BLK:].astype(BF)
        if pair == 0:
            dk[: 6 * BLK, :] = dkw
            dv[: 6 * BLK, :] = dvw
        else:
            dk[2 * BLK : 6 * BLK, :] += dkw[: 4 * BLK]
            dv[2 * BLK : 6 * BLK, :] += dvw[: 4 * BLK]
            dk[6 * BLK :, :] = dkw[4 * BLK :]
            dv[6 * BLK :, :] = dvw[4 * BLK :]
    for s, o in enumerate((dq0, dq1, dq2, dq3)):
        o[...] = dqs[lax.rem(z + s, NZ)]
    for j in range(2):
        rim_before[j, 0] = (dk[j * BLK : (j + 1) * BLK, :] * SCALE).astype(BF)
        rim_before[j, 1] = dv[j * BLK : (j + 1) * BLK, :].astype(BF)
        rim_after[j, 0] = (dk[(6 + j) * BLK : (7 + j) * BLK, :] * SCALE).astype(BF)
        rim_after[j, 1] = dv[(6 + j) * BLK : (7 + j) * BLK, :].astype(BF)
    for j in range(4):
        own[j, 0] = dk[(2 + j) * BLK : (3 + j) * BLK, :] * SCALE
        own[j, 1] = dv[(2 + j) * BLK : (3 + j) * BLK, :]


def attend(zh, q, g, recv, before, lo, hi, after, bias, first, heads, group):
    n = heads * HD
    mine = pl.BlockSpec((BLK, HD), lambda h, z: (0, z[0] * group + first + h))
    two = pl.BlockSpec((2, BLK, HD), lambda h, z: (0, 0, h))
    one = pl.BlockSpec((1, BLK, HD), lambda h, z: (0, 0, h))
    flat = pl.BlockSpec((BLK, HD), lambda h, z: (0, h))
    rim = pl.BlockSpec((2, 2, BLK, HD), lambda h, z: (0, 0, 0, h))
    own = pl.BlockSpec((4, 2, BLK, HD), lambda h, z: (0, 0, 0, h))
    shape = jax.ShapeDtypeStruct
    return pl.pallas_call(
        attend_body,
        grid_spec=pltpu.PrefetchScalarGridSpec(
            num_scalar_prefetch=1,
            grid=(heads,),
            in_specs=[mine, mine, two, two, one, one, rim, rim, rim, rim,
                      pl.BlockSpec((1, 2, 6, 2 * BLK), lambda h, z: (first + h, 0, 0, 0))],
            out_specs=[flat] * 4 + [rim, rim, own],
            scratch_shapes=[
                pltpu.VMEM((4 * BLK, HD), BF),
                pltpu.VMEM((4 * BLK, HD), BF),
                pltpu.VMEM((8 * BLK, HD), BF),
                pltpu.VMEM((8 * BLK, HD), BF),
                pltpu.VMEM((4, BLK, HD), BF),
                pltpu.VMEM((8 * BLK, HD), F32),
                pltpu.VMEM((8 * BLK, HD), F32),
            ],
        ),
        out_shape=[shape((BLK, n), BF)] * 4
        + [shape((2, 2, BLK, n), BF)] * 2
        + [shape((4, 2, BLK, n), F32)],
        cost_estimate=cost(heads * 2 * 5 * 2 * 768 * 256 * 128, 40 * BLK * n * 2),
        compiler_params=grant(24),
    )(zh, q, g, *recv, before, lo, hi, after, bias)


def finish_body(zh, own, from_before, from_after, o0, o1, o2, o3):
    z = zh[0]
    for s, o in enumerate((o0, o1, o2, o3)):
        b = lax.rem(z + s, NZ)

        @pl.when(b < 2)
        def _():
            o[...] = (own[b] + from_before[b].astype(F32)).astype(BF)

        @pl.when(b >= 2)
        def _():
            o[...] = (own[b] + from_after[b - 2].astype(F32)).astype(BF)


def finish(zh, own, from_before, from_after):
    n = own.shape[-1]
    rim = pl.BlockSpec((2, 2, BLK, CW), lambda i, z: (0, 0, 0, i))
    out = pl.BlockSpec((2, BLK, CW), lambda i, z: (0, 0, i))
    return pl.pallas_call(
        finish_body,
        grid_spec=pltpu.PrefetchScalarGridSpec(
            num_scalar_prefetch=1,
            grid=(n // CW,),
            in_specs=[pl.BlockSpec((4, 2, BLK, CW), lambda i, z: (0, 0, 0, i)), rim, rim],
            out_specs=[out] * 4,
        ),
        out_shape=[jax.ShapeDtypeStruct((2, BLK, n), BF)] * 4,
        cost_estimate=cost(0, 32 * BLK * n * 2),
        compiler_params=grant(12),
    )(zh, own, from_before, from_after)


def assemble_body(zh, *refs):
    n_chunks = len(CHUNKS)
    ins, outs = refs[: 8 * n_chunks], refs[8 * n_chunks :]
    t = pl.program_id(0)
    for s in range(NZ):

        @pl.when(t == s)
        def _():
            for c, (first, heads) in enumerate(CHUNKS):
                cols = slice(first * HD, (first + heads) * HD)
                outs[0][:, cols] = ins[8 * c + s][...]
                outs[1][:, cols] = ins[8 * c + 4 + s][0]
                outs[2][:, cols] = ins[8 * c + 4 + s][1]


def assemble(zh, parts, group, width):
    specs, args = [], []
    for dq, dkv in parts:
        for a in (*dq, *dkv):
            specs.append(pl.BlockSpec(a.shape, lambda t, z, nd=a.ndim: (0,) * nd))
            args.append(a)
    out = pl.BlockSpec((BLK, group * HD), lambda t, z: (0, lax.rem(z[0] + NZ - t, NZ)))
    return pl.pallas_call(
        assemble_body,
        grid_spec=pltpu.PrefetchScalarGridSpec(
            num_scalar_prefetch=1, grid=(NZ,), in_specs=specs, out_specs=[out] * 3
        ),
        out_shape=[jax.ShapeDtypeStruct((BLK, width), BF)] * 3,
        cost_estimate=cost(0, 6 * BLK * width * 2),
        compiler_params=grant(24),
        name="assemble",
    )(zh, *args)


def tile_bias(tile_mask, zh, slab, group):
    all_blocks, span = tile_mask.shape[1], tile_mask.shape[2]
    local = lax.dynamic_slice(tile_mask, (zh * group, slab * NZ, 0), (group, NZ, span))
    key_block = slab * NZ + jnp.arange(NZ, dtype=jnp.int32)[:, None] + jnp.arange(span, dtype=jnp.int32)[None] - span // 2
    active = (local != 0) & (key_block >= 0) & (key_block < all_blocks)
    active = active.reshape(group, 2, 2, span)
    left = jnp.pad(active[:, :, 0], ((0, 0), (0, 0), (0, 1)))
    right = jnp.pad(active[:, :, 1], ((0, 0), (0, 0), (1, 0)))
    rows = jnp.stack([left, right], -1)
    return jnp.repeat(jnp.where(rows, 0.0, -jnp.inf).astype(F32), BLK, axis=-1)


def shards(query, key, value, dout, tile_mask):
    n_ctx, n_uly = lax.axis_size("ctx"), lax.axis_size("uly")
    width = query.shape[1]
    group = tile_mask.shape[0] // NZ
    me = lax.axis_index("uly")
    zh_s = lax.rem(me, NZ)
    slab = lax.axis_index("ctx") * (n_uly // NZ) + me // NZ
    zh = zh_s.astype(jnp.int32).reshape(1)
    n_slabs = n_ctx * n_uly // NZ
    rings = [
        [(NZ * i + j, NZ * i + (j + s) % NZ) for i in range(n_uly // NZ) for j in range(NZ)] for s in range(NZ)
    ]
    up = [(NZ * i + j, NZ * (i + 1) + j) for i in range(n_slabs - 1) for j in range(NZ)]
    down = [(b, a) for a, b in up]

    def move(axes, perm, a):
        return lax.ppermute(a, axes, perm)

    def around(arrays):
        return [move("uly", rings[s], a) for s, a in enumerate(arrays, 1)]

    def to_next(a):
        return move(("ctx", "uly"), up, a)

    def to_prev(a):
        return move(("ctx", "uly"), down, a)

    bias = tile_bias(tile_mask, zh_s, slab, group)

    def gather(a, b, first, heads, wide):
        rp, rm = pack(zh, ((a, 2),), ((b, 2),), first, heads, group, wide)
        mp, mm = pack(zh, ((a, 1), (b, 1)), ((a, 3), (b, 3)), first, heads, group, wide)
        rp, rm = move("uly", rings[1], rp), move("uly", rings[3], rm)
        mp, mm = move("uly", rings[1], mp), move("uly", rings[3], mm)
        fp, fm = move("uly", rings[1], rp), move("uly", rings[3], rm)
        return mp, mm, fp, fm

    kv = gather(key, value, 0, group, group * HD // 2)
    qg = [gather(query, dout, first, heads, CW) for first, heads in CHUNKS]
    parts = []
    for c, (first, heads) in enumerate(CHUNKS):
        recv = qg[c]
        lo, hi = unpack(zh, key, value, kv, first, heads, group)
        before, after = to_next(hi), to_prev(lo)
        *dq, rim_before, rim_after, own = attend(
            zh, query, dout, recv, before, lo, hi, after, bias, first, heads, group
        )
        from_after, from_before = to_prev(rim_before), to_next(rim_after)
        back_q = [dq[0], *around(dq[1:])]
        dkv = finish(zh, own, from_before, from_after)
        back_kv = [dkv[0], *around(dkv[1:])]
        parts.append((back_q, back_kv))
    return assemble(zh, parts, group, width)


def solution(mesh):
    rows = P(("ctx", "uly"), None)
    return jax.shard_map(
        shards,
        mesh=mesh,
        in_specs=(rows, rows, rows, rows, P()),
        out_specs=(rows, rows, rows),
        check_vma=False,
    )
```

```python
import functools
import math

import jax
import jax.numpy as jnp
from jax import lax
from jax.experimental import pallas as pl
from jax.experimental.pallas import tpu as pltpu
from jax.sharding import PartitionSpec as P


BLK = 128
HD = 128
NZ = 4
CHUNKS = ((0, 4), (4, 6))
CW = 256
SCALE = 1.0 / math.sqrt(HD)
EXP2_SCALE = SCALE / math.log(2.0)
BF = jnp.bfloat16
F32 = jnp.float32


MIB = 1 << 20


def grant(mib):
    return pltpu.CompilerParams(vmem_limit_bytes=mib * MIB)


def cost(flops, nbytes):
    return pl.CostEstimate(flops=flops, bytes_accessed=nbytes, transcendentals=0)


def pack_direct_body(zh, a1, a2, a3, b1, b2, b3, o1, o2, o3):
    for a, b, o in ((a1, b1, o1), (a2, b2, o2), (a3, b3, o3)):
        o[0] = a[...]
        o[1] = b[...]


def pack_direct(zh, a, b, first, heads, group):
    per, off, steps = group * HD // CW, first * HD // CW, heads * HD // CW

    def src(s):
        return pl.BlockSpec((BLK, CW), lambda i, z: (0, lax.rem(z[0] + s, NZ) * per + off + i))

    out = pl.BlockSpec((2, BLK, CW), lambda i, z: (0, 0, i))
    return pl.pallas_call(
        pack_direct_body,
        grid_spec=pltpu.PrefetchScalarGridSpec(
            num_scalar_prefetch=1,
            grid=(steps,),
            in_specs=[src(1), src(2), src(3)] * 2,
            out_specs=[out] * 3,
        ),
        out_shape=[jax.ShapeDtypeStruct((2, BLK, heads * HD), BF)] * 3,
        cost_estimate=cost(0, 12 * BLK * heads * HD * 2),
        compiler_params=grant(56),
    )(zh, a, a, a, b, b, b)


def pack_body(zh, *refs):
    ins, (plus, minus) = refs[:-2], refs[-2:]
    m = len(ins) // 2
    for i in range(m):
        plus[i] = ins[i][...]
        minus[i] = ins[m + i][...]


def pack(zh, plus, minus, first, heads, group, wide=CW):
    per, off, steps = group * HD // wide, first * HD // wide, heads * HD // wide
    n, m = heads * HD, len(plus)

    def src(s):
        return pl.BlockSpec((BLK, wide), lambda i, z: (0, lax.rem(z[0] + s, NZ) * per + off + i))

    out = pl.BlockSpec((m, BLK, wide), lambda i, z: (0, 0, i))
    return pl.pallas_call(
        pack_body,
        grid_spec=pltpu.PrefetchScalarGridSpec(
            num_scalar_prefetch=1,
            grid=(steps,),
            in_specs=[src(s) for _, s in (*plus, *minus)],
            out_specs=[out, out],
        ),
        out_shape=[jax.ShapeDtypeStruct((m, BLK, n), BF)] * 2,
        cost_estimate=cost(0, 4 * m * BLK * n * 2),
        compiler_params=grant(56),
    )(zh, *[a for a, _ in (*plus, *minus)])


def unpack_body(zh, k, v, mp, mm, fp, fm, *halves):
    z, step = zh[0], pl.program_id(0)
    parts = ((k, v), (mp.at[0], mp.at[1]), (fp.at[0], fm.at[0]), (mm.at[0], mm.at[1]))
    for c, (first, heads) in enumerate(CHUNKS):
        lo, hi = halves[2 * c : 2 * c + 2]

        @pl.when((step >= first * HD // CW) & (step < (first + heads) * HD // CW))
        def _():
            for s, (kk, vv) in enumerate(parts):
                b = lax.rem(z + NZ - s, NZ)

                @pl.when(b < 2)
                def _():
                    lo[b, 0] = kk[...]
                    lo[b, 1] = vv[...]

                @pl.when(b >= 2)
                def _():
                    hi[b - 2, 0] = kk[...]
                    hi[b - 2, 1] = vv[...]


def unpack(zh, k, v, recv, group):
    per = group * HD // CW
    own = pl.BlockSpec((BLK, CW), lambda i, z: (0, z[0] * per + i))
    two = pl.BlockSpec((2, BLK, CW), lambda i, z: (0, 0, i))
    one = pl.BlockSpec((1, BLK, CW), lambda i, z: (0, 0, i))
    specs, shapes = [], []
    for first, heads in CHUNKS:
        lo, n = first * HD // CW, heads * HD // CW
        half = pl.BlockSpec(
            (2, 2, BLK, CW), lambda i, z, lo=lo, n=n: (0, 0, 0, jnp.minimum(jnp.maximum(i - lo, 0), n - 1))
        )
        specs += [half, half]
        shapes += [jax.ShapeDtypeStruct((2, 2, BLK, heads * HD), BF)] * 2
    return pl.pallas_call(
        unpack_body,
        grid_spec=pltpu.PrefetchScalarGridSpec(
            num_scalar_prefetch=1, grid=(per,), in_specs=[own, own, two, two, one, one], out_specs=specs
        ),
        out_shape=shapes,
        cost_estimate=cost(0, 16 * BLK * group * HD * 2),
        compiler_params=grant(12),
        name="unpack",
    )(zh, k, v, *recv)


def attend_body(direct, zh, q0, g0, *refs):
    n = 3 if direct else 4
    got, refs = refs[:n], refs[n:]
    before, lo, hi, after, bias, *refs = refs
    if direct:
        one, two, three = ((r.at[0], r.at[1]) for r in got)
    else:
        mp, mm, fp, fm = got
        one, two, three = (mp.at[0], mp.at[1]), (fp.at[0], fm.at[0]), (mm.at[0], mm.at[1])
    (
        dq0, dq1, dq2, dq3, rim_before, rim_after, own,
        qs, gs, ks, vs, dqs, dk, dv,
    ) = refs
    z = zh[0]
    for s, (qq, gg) in enumerate(((q0, g0), one, two, three)):
        row = pl.multiple_of(lax.rem(z + NZ - s, NZ) * BLK, BLK)
        qs[pl.ds(row, BLK), :] = qq[...]
        gs[pl.ds(row, BLK), :] = gg[...]
    for i, (ref, j) in enumerate(
        ((before, 0), (before, 1), (lo, 0), (lo, 1), (hi, 0), (hi, 1), (after, 0), (after, 1))
    ):
        ks[i * BLK : (i + 1) * BLK, :] = ref[j, 0]
        vs[i * BLK : (i + 1) * BLK, :] = ref[j, 1]
    nt = (((1,), (1,)), ((), ()))
    tn = (((0,), (0,)), ((), ()))
    nn = (((1,), (0,)), ((), ()))
    for pair in range(2):
        r0 = pair * 2 * BLK
        kw, vw = ks[r0 : r0 + 6 * BLK, :], vs[r0 : r0 + 6 * BLK, :]
        q, g = qs[r0 : r0 + 2 * BLK, :], gs[r0 : r0 + 2 * BLK, :]
        st = lax.dot_general(kw, q, nt, preferred_element_type=F32)
        st = st.reshape(6, BLK, 2 * BLK) + bias[0, pair][:, None, :]
        top = jnp.max(jnp.max(st, axis=0), axis=0, keepdims=True)[None]
        e = jnp.exp2((st - top) * EXP2_SCALE)
        total = jnp.sum(jnp.sum(e, axis=0), axis=0, keepdims=True)[None]
        p = e * (1.0 / total)
        dp = lax.dot_general(vw, g, nt, preferred_element_type=F32).reshape(6, BLK, 2 * BLK)
        delta = jnp.sum(jnp.sum(p * dp, axis=0), axis=0, keepdims=True)[None]
        ds = (p * (dp - delta)).astype(BF).reshape(6 * BLK, 2 * BLK)
        pb = p.astype(BF).reshape(6 * BLK, 2 * BLK)
        dvw = lax.dot_general(pb, g, nn, preferred_element_type=F32)
        dkw = lax.dot_general(ds, q, nn, preferred_element_type=F32)
        dqw = lax.dot_general(ds, kw, tn, preferred_element_type=F32) * SCALE
        dqs[2 * pair] = dqw[:BLK].astype(BF)
        dqs[2 * pair + 1] = dqw[BLK:].astype(BF)
        if pair == 0:
            dk[: 6 * BLK, :] = dkw
            dv[: 6 * BLK, :] = dvw
        else:
            dk[2 * BLK : 6 * BLK, :] += dkw[: 4 * BLK]
            dv[2 * BLK : 6 * BLK, :] += dvw[: 4 * BLK]
            dk[6 * BLK :, :] = dkw[4 * BLK :]
            dv[6 * BLK :, :] = dvw[4 * BLK :]
    for s, o in enumerate((dq0, dq1, dq2, dq3)):
        o[...] = dqs[lax.rem(z + s, NZ)]
    for j in range(2):
        rim_before[j, 0] = (dk[j * BLK : (j + 1) * BLK, :] * SCALE).astype(BF)
        rim_before[j, 1] = dv[j * BLK : (j + 1) * BLK, :].astype(BF)
        rim_after[j, 0] = (dk[(6 + j) * BLK : (7 + j) * BLK, :] * SCALE).astype(BF)
        rim_after[j, 1] = dv[(6 + j) * BLK : (7 + j) * BLK, :].astype(BF)
    for j in range(4):
        own[j, 0] = dk[(2 + j) * BLK : (3 + j) * BLK, :] * SCALE
        own[j, 1] = dv[(2 + j) * BLK : (3 + j) * BLK, :]


def attend(zh, q, g, recv, before, lo, hi, after, bias, first, heads, group):
    n = heads * HD
    mine = pl.BlockSpec((BLK, HD), lambda h, z: (0, z[0] * group + first + h))
    two = pl.BlockSpec((2, BLK, HD), lambda h, z: (0, 0, h))
    one = pl.BlockSpec((1, BLK, HD), lambda h, z: (0, 0, h))
    direct = len(recv) == 3
    got = [two] * 3 if direct else [two, two, one, one]
    flat = pl.BlockSpec((BLK, HD), lambda h, z: (0, h))
    rim = pl.BlockSpec((2, 2, BLK, HD), lambda h, z: (0, 0, 0, h))
    own = pl.BlockSpec((4, 2, BLK, HD), lambda h, z: (0, 0, 0, h))
    shape = jax.ShapeDtypeStruct
    return pl.pallas_call(
        functools.partial(attend_body, direct),
        grid_spec=pltpu.PrefetchScalarGridSpec(
            num_scalar_prefetch=1,
            grid=(heads,),
            in_specs=[mine, mine, *got, rim, rim, rim, rim,
                      pl.BlockSpec((1, 2, 6, 2 * BLK), lambda h, z: (first + h, 0, 0, 0))],
            out_specs=[flat] * 4 + [rim, rim, own],
            scratch_shapes=[
                pltpu.VMEM((4 * BLK, HD), BF),
                pltpu.VMEM((4 * BLK, HD), BF),
                pltpu.VMEM((8 * BLK, HD), BF),
                pltpu.VMEM((8 * BLK, HD), BF),
                pltpu.VMEM((4, BLK, HD), BF),
                pltpu.VMEM((8 * BLK, HD), F32),
                pltpu.VMEM((8 * BLK, HD), F32),
            ],
        ),
        out_shape=[shape((BLK, n), BF)] * 4
        + [shape((2, 2, BLK, n), BF)] * 2
        + [shape((4, 2, BLK, n), F32)],
        cost_estimate=cost(heads * 2 * 5 * 2 * 768 * 256 * 128, 40 * BLK * n * 2),
        compiler_params=grant(24),
    )(zh, q, g, *recv, before, lo, hi, after, bias)


def finish_body(zh, own, from_before, from_after, o0, o1, o2, o3):
    z = zh[0]
    for s, o in enumerate((o0, o1, o2, o3)):
        b = lax.rem(z + s, NZ)

        @pl.when(b < 2)
        def _():
            o[...] = (own[b] + from_before[b].astype(F32)).astype(BF)

        @pl.when(b >= 2)
        def _():
            o[...] = (own[b] + from_after[b - 2].astype(F32)).astype(BF)


def finish(zh, own, from_before, from_after):
    n = own.shape[-1]
    rim = pl.BlockSpec((2, 2, BLK, CW), lambda i, z: (0, 0, 0, i))
    out = pl.BlockSpec((2, BLK, CW), lambda i, z: (0, 0, i))
    return pl.pallas_call(
        finish_body,
        grid_spec=pltpu.PrefetchScalarGridSpec(
            num_scalar_prefetch=1,
            grid=(n // CW,),
            in_specs=[pl.BlockSpec((4, 2, BLK, CW), lambda i, z: (0, 0, 0, i)), rim, rim],
            out_specs=[out] * 4,
        ),
        out_shape=[jax.ShapeDtypeStruct((2, BLK, n), BF)] * 4,
        cost_estimate=cost(0, 32 * BLK * n * 2),
        compiler_params=grant(12),
    )(zh, own, from_before, from_after)


def assemble_body(zh, *refs):
    n_chunks = len(CHUNKS)
    ins, outs = refs[: 8 * n_chunks], refs[8 * n_chunks :]
    t = pl.program_id(0)
    for s in range(NZ):

        @pl.when(t == s)
        def _():
            for c, (first, heads) in enumerate(CHUNKS):
                cols = slice(first * HD, (first + heads) * HD)
                outs[0][:, cols] = ins[8 * c + s][...]
                outs[1][:, cols] = ins[8 * c + 4 + s][0]
                outs[2][:, cols] = ins[8 * c + 4 + s][1]


def assemble(zh, parts, group, width):
    specs, args = [], []
    for dq, dkv in parts:
        for a in (*dq, *dkv):
            specs.append(pl.BlockSpec(a.shape, lambda t, z, nd=a.ndim: (0,) * nd))
            args.append(a)
    out = pl.BlockSpec((BLK, group * HD), lambda t, z: (0, lax.rem(z[0] + NZ - t, NZ)))
    return pl.pallas_call(
        assemble_body,
        grid_spec=pltpu.PrefetchScalarGridSpec(
            num_scalar_prefetch=1, grid=(NZ,), in_specs=specs, out_specs=[out] * 3
        ),
        out_shape=[jax.ShapeDtypeStruct((BLK, width), BF)] * 3,
        cost_estimate=cost(0, 6 * BLK * width * 2),
        compiler_params=grant(24),
        name="assemble",
    )(zh, *args)


def tile_bias(tile_mask, zh, slab, group):
    all_blocks, span = tile_mask.shape[1], tile_mask.shape[2]
    local = lax.dynamic_slice(tile_mask, (zh * group, slab * NZ, 0), (group, NZ, span))
    key_block = slab * NZ + jnp.arange(NZ, dtype=jnp.int32)[:, None] + jnp.arange(span, dtype=jnp.int32)[None] - span // 2
    active = (local != 0) & (key_block >= 0) & (key_block < all_blocks)
    active = active.reshape(group, 2, 2, span)
    left = jnp.pad(active[:, :, 0], ((0, 0), (0, 0), (0, 1)))
    right = jnp.pad(active[:, :, 1], ((0, 0), (0, 0), (1, 0)))
    rows = jnp.stack([left, right], -1)
    return jnp.repeat(jnp.where(rows, 0.0, -jnp.inf).astype(F32), BLK, axis=-1)


def shards(query, key, value, dout, tile_mask):
    n_ctx, n_uly = lax.axis_size("ctx"), lax.axis_size("uly")
    width = query.shape[1]
    group = tile_mask.shape[0] // NZ
    me = lax.axis_index("uly")
    zh_s = lax.rem(me, NZ)
    slab = lax.axis_index("ctx") * (n_uly // NZ) + me // NZ
    zh = zh_s.astype(jnp.int32).reshape(1)
    n_slabs = n_ctx * n_uly // NZ
    rings = [
        [(NZ * i + j, NZ * i + (j + s) % NZ) for i in range(n_uly // NZ) for j in range(NZ)] for s in range(NZ)
    ]
    up = [(NZ * i + j, NZ * (i + 1) + j) for i in range(n_slabs - 1) for j in range(NZ)]
    down = [(b, a) for a, b in up]

    def move(axes, perm, a):
        return lax.ppermute(a, axes, perm)

    def around(arrays):
        return [move("uly", rings[s], a) for s, a in enumerate(arrays, 1)]

    def to_next(a):
        return move(("ctx", "uly"), up, a)

    def to_prev(a):
        return move(("ctx", "uly"), down, a)

    key, value, query, dout = (pltpu.with_memory_space_constraint(a, pltpu.HBM) for a in (key, value, query, dout))
    bias = tile_bias(tile_mask, zh_s, slab, group)

    def gather(a, b, first, heads, wide):
        rp, rm = pack(zh, ((a, 2),), ((b, 2),), first, heads, group, wide)
        mp, mm = pack(zh, ((a, 1), (b, 1)), ((a, 3), (b, 3)), first, heads, group, wide)
        rp, rm = move("uly", rings[1], rp), move("uly", rings[3], rm)
        mp, mm = move("uly", rings[1], mp), move("uly", rings[3], mm)
        fp, fm = move("uly", rings[1], rp), move("uly", rings[3], rm)
        return mp, mm, fp, fm

    kv = gather(key, value, 0, group, group * HD // 2)
    qg = [gather(query, dout, *CHUNKS[0], CW), around(pack_direct(zh, query, dout, *CHUNKS[1], group))]
    halves = unpack(zh, key, value, kv, group)
    parts = []
    for c, (first, heads) in enumerate(CHUNKS):
        recv = qg[c]
        lo, hi = halves[2 * c : 2 * c + 2]
        before, after = to_next(hi), to_prev(lo)
        *dq, rim_before, rim_after, own = attend(
            zh, query, dout, recv, before, lo, hi, after, bias, first, heads, group
        )
        from_after, from_before = to_prev(rim_before), to_next(rim_after)
        back_q = [dq[0], *around(dq[1:])]
        dkv = finish(zh, own, from_before, from_after)
        back_kv = [dkv[0], *around(dkv[1:])]
        parts.append((back_q, back_kv))
    return assemble(zh, parts, group, width)


def solution(mesh):
    rows = P(("ctx", "uly"), None)
    return jax.shard_map(
        shards,
        mesh=mesh,
        in_specs=(rows, rows, rows, rows, P()),
        out_specs=(rows, rows, rows),
        check_vma=False,
    )
```

```python
import math

import jax
import jax.numpy as jnp
from jax import lax
from jax.experimental import pallas as pl
from jax.experimental.pallas import tpu as pltpu
from jax.sharding import PartitionSpec as P


BLK = 128
HD = 128
NZ = 4
CHUNKS = ((0, 6), (6, 4))
CW = 256
SCALE = 1.0 / math.sqrt(HD)
EXP2_SCALE = SCALE / math.log(2.0)
BF = jnp.bfloat16
F32 = jnp.float32


MIB = 1 << 20


def grant(mib):
    return pltpu.CompilerParams(vmem_limit_bytes=mib * MIB)


def cost(flops, nbytes):
    return pl.CostEstimate(flops=flops, bytes_accessed=nbytes, transcendentals=0)


def pack_body(zh, *refs):
    ins, (plus, minus) = refs[:-2], refs[-2:]
    m = len(ins) // 2
    for i in range(m):
        plus[i] = ins[i][...]
        minus[i] = ins[m + i][...]


def pack(zh, plus, minus, first, heads, group, wide=CW):
    per, off, steps = group * HD // wide, first * HD // wide, heads * HD // wide
    n, m = heads * HD, len(plus)

    def src(s):
        return pl.BlockSpec((BLK, wide), lambda i, z: (0, lax.rem(z[0] + s, NZ) * per + off + i))

    out = pl.BlockSpec((m, BLK, wide), lambda i, z: (0, 0, i))
    return pl.pallas_call(
        pack_body,
        grid_spec=pltpu.PrefetchScalarGridSpec(
            num_scalar_prefetch=1,
            grid=(steps,),
            in_specs=[src(s) for _, s in (*plus, *minus)],
            out_specs=[out, out],
        ),
        out_shape=[jax.ShapeDtypeStruct((m, BLK, n), BF)] * 2,
        cost_estimate=cost(0, 4 * m * BLK * n * 2),
        compiler_params=grant(56),
    )(zh, *[a for a, _ in (*plus, *minus)])


def unpack_body(zh, k, v, mp, mm, fp, fm, *halves):
    z, step = zh[0], pl.program_id(0)
    parts = ((k, v), (mp.at[0], mp.at[1]), (fp.at[0], fm.at[0]), (mm.at[0], mm.at[1]))
    for c, (first, heads) in enumerate(CHUNKS):
        lo, hi = halves[2 * c : 2 * c + 2]

        @pl.when((step >= first * HD // CW) & (step < (first + heads) * HD // CW))
        def _():
            for s, (kk, vv) in enumerate(parts):
                b = lax.rem(z + NZ - s, NZ)

                @pl.when(b < 2)
                def _():
                    lo[b, 0] = kk[...]
                    lo[b, 1] = vv[...]

                @pl.when(b >= 2)
                def _():
                    hi[b - 2, 0] = kk[...]
                    hi[b - 2, 1] = vv[...]


def unpack(zh, k, v, recv, group):
    per = group * HD // CW
    own = pl.BlockSpec((BLK, CW), lambda i, z: (0, z[0] * per + i))
    two = pl.BlockSpec((2, BLK, CW), lambda i, z: (0, 0, i))
    one = pl.BlockSpec((1, BLK, CW), lambda i, z: (0, 0, i))
    specs, shapes = [], []
    for first, heads in CHUNKS:
        lo, n = first * HD // CW, heads * HD // CW
        half = pl.BlockSpec(
            (2, 2, BLK, CW), lambda i, z, lo=lo, n=n: (0, 0, 0, jnp.minimum(jnp.maximum(i - lo, 0), n - 1))
        )
        specs += [half, half]
        shapes += [jax.ShapeDtypeStruct((2, 2, BLK, heads * HD), BF)] * 2
    return pl.pallas_call(
        unpack_body,
        grid_spec=pltpu.PrefetchScalarGridSpec(
            num_scalar_prefetch=1, grid=(per,), in_specs=[own, own, two, two, one, one], out_specs=specs
        ),
        out_shape=shapes,
        cost_estimate=cost(0, 16 * BLK * group * HD * 2),
        compiler_params=grant(12),
        name="unpack",
    )(zh, k, v, *recv)


def attend_body(zh, q0, g0, mp, mm, fp, fm, before, lo, hi, after, bias,
                dq0, dq1, dq2, dq3, rim_before, rim_after, own,
                qs, gs, ks, vs, dqs, dk, dv):
    a = mp.shape[0] - 2
    one, two, three = (mp.at[a], mp.at[a + 1]), (fp.at[0], fm.at[0]), (mm.at[a], mm.at[a + 1])
    z = zh[0]
    for s, (qq, gg) in enumerate(((q0, g0), one, two, three)):
        row = pl.multiple_of(lax.rem(z + NZ - s, NZ) * BLK, BLK)
        qs[pl.ds(row, BLK), :] = qq[...]
        gs[pl.ds(row, BLK), :] = gg[...]
    for i, (ref, j) in enumerate(
        ((before, 0), (before, 1), (lo, 0), (lo, 1), (hi, 0), (hi, 1), (after, 0), (after, 1))
    ):
        ks[i * BLK : (i + 1) * BLK, :] = ref[j, 0]
        vs[i * BLK : (i + 1) * BLK, :] = ref[j, 1]
    nt = (((1,), (1,)), ((), ()))
    tn = (((0,), (0,)), ((), ()))
    nn = (((1,), (0,)), ((), ()))
    for pair in range(2):
        r0 = pair * 2 * BLK
        kw, vw = ks[r0 : r0 + 6 * BLK, :], vs[r0 : r0 + 6 * BLK, :]
        q, g = qs[r0 : r0 + 2 * BLK, :], gs[r0 : r0 + 2 * BLK, :]
        st = lax.dot_general(kw, q, nt, preferred_element_type=F32)
        st = st.reshape(6, BLK, 2 * BLK) + bias[0, pair][:, None, :]
        top = jnp.max(jnp.max(st, axis=0), axis=0, keepdims=True)[None]
        e = jnp.exp2((st - top) * EXP2_SCALE)
        total = jnp.sum(jnp.sum(e, axis=0), axis=0, keepdims=True)[None]
        p = e * (1.0 / total)
        dp = lax.dot_general(vw, g, nt, preferred_element_type=F32).reshape(6, BLK, 2 * BLK)
        delta = jnp.sum(jnp.sum(p * dp, axis=0), axis=0, keepdims=True)[None]
        ds = (p * (dp - delta)).astype(BF).reshape(6 * BLK, 2 * BLK)
        pb = p.astype(BF).reshape(6 * BLK, 2 * BLK)
        dvw = lax.dot_general(pb, g, nn, preferred_element_type=F32)
        dkw = lax.dot_general(ds, q, nn, preferred_element_type=F32)
        dqw = lax.dot_general(ds, kw, tn, preferred_element_type=F32) * SCALE
        dqs[2 * pair] = dqw[:BLK].astype(BF)
        dqs[2 * pair + 1] = dqw[BLK:].astype(BF)
        if pair == 0:
            dk[: 6 * BLK, :] = dkw
            dv[: 6 * BLK, :] = dvw
        else:
            dk[2 * BLK : 6 * BLK, :] += dkw[: 4 * BLK]
            dv[2 * BLK : 6 * BLK, :] += dvw[: 4 * BLK]
            dk[6 * BLK :, :] = dkw[4 * BLK :]
            dv[6 * BLK :, :] = dvw[4 * BLK :]
    for s, o in enumerate((dq0, dq1, dq2, dq3)):
        o[...] = dqs[lax.rem(z + s, NZ)]
    for j in range(2):
        rim_before[j, 0] = (dk[j * BLK : (j + 1) * BLK, :] * SCALE).astype(BF)
        rim_before[j, 1] = dv[j * BLK : (j + 1) * BLK, :].astype(BF)
        rim_after[j, 0] = (dk[(6 + j) * BLK : (7 + j) * BLK, :] * SCALE).astype(BF)
        rim_after[j, 1] = dv[(6 + j) * BLK : (7 + j) * BLK, :].astype(BF)
    for j in range(4):
        own[j, 0] = dk[(2 + j) * BLK : (3 + j) * BLK, :] * SCALE
        own[j, 1] = dv[(2 + j) * BLK : (3 + j) * BLK, :]


def attend(zh, q, g, recv, before, lo, hi, after, bias, first, heads, group):
    n = heads * HD
    mine = pl.BlockSpec((BLK, HD), lambda h, z: (0, z[0] * group + first + h))
    got = [pl.BlockSpec((a.shape[0], BLK, HD), lambda h, z: (0, 0, h)) for a in recv]
    flat = pl.BlockSpec((BLK, HD), lambda h, z: (0, h))
    rim = pl.BlockSpec((2, 2, BLK, HD), lambda h, z: (0, 0, 0, h))
    own = pl.BlockSpec((4, 2, BLK, HD), lambda h, z: (0, 0, 0, h))
    shape = jax.ShapeDtypeStruct
    return pl.pallas_call(
        attend_body,
        grid_spec=pltpu.PrefetchScalarGridSpec(
            num_scalar_prefetch=1,
            grid=(heads,),
            in_specs=[mine, mine, *got, rim, rim, rim, rim,
                      pl.BlockSpec((1, 2, 6, 2 * BLK), lambda h, z: (first + h, 0, 0, 0))],
            out_specs=[flat] * 4 + [rim, rim, own],
            scratch_shapes=[
                pltpu.VMEM((4 * BLK, HD), BF),
                pltpu.VMEM((4 * BLK, HD), BF),
                pltpu.VMEM((8 * BLK, HD), BF),
                pltpu.VMEM((8 * BLK, HD), BF),
                pltpu.VMEM((4, BLK, HD), BF),
                pltpu.VMEM((8 * BLK, HD), F32),
                pltpu.VMEM((8 * BLK, HD), F32),
            ],
        ),
        out_shape=[shape((BLK, n), BF)] * 4
        + [shape((2, 2, BLK, n), BF)] * 2
        + [shape((4, 2, BLK, n), F32)],
        cost_estimate=cost(heads * 2 * 5 * 2 * 768 * 256 * 128, 40 * BLK * n * 2),
        compiler_params=grant(24),
    )(zh, q, g, *recv, before, lo, hi, after, bias)


def finish_body(zh, own, from_before, from_after, o0, o1, o2, o3):
    z = zh[0]
    for s, o in enumerate((o0, o1, o2, o3)):
        b = lax.rem(z + s, NZ)

        @pl.when(b < 2)
        def _():
            o[...] = (own[b] + from_before[b].astype(F32)).astype(BF)

        @pl.when(b >= 2)
        def _():
            o[...] = (own[b] + from_after[b - 2].astype(F32)).astype(BF)


def finish(zh, own, from_before, from_after):
    n = own.shape[-1]
    rim = pl.BlockSpec((2, 2, BLK, CW), lambda i, z: (0, 0, 0, i))
    out = pl.BlockSpec((2, BLK, CW), lambda i, z: (0, 0, i))
    return pl.pallas_call(
        finish_body,
        grid_spec=pltpu.PrefetchScalarGridSpec(
            num_scalar_prefetch=1,
            grid=(n // CW,),
            in_specs=[pl.BlockSpec((4, 2, BLK, CW), lambda i, z: (0, 0, 0, i)), rim, rim],
            out_specs=[out] * 4,
        ),
        out_shape=[jax.ShapeDtypeStruct((2, BLK, n), BF)] * 4,
        cost_estimate=cost(0, 32 * BLK * n * 2),
        compiler_params=grant(12),
    )(zh, own, from_before, from_after)


def assemble_body(zh, *refs):
    n_chunks = len(CHUNKS)
    ins, outs = refs[: 8 * n_chunks], refs[8 * n_chunks :]
    t = pl.program_id(0)
    for s in range(NZ):

        @pl.when(t == s)
        def _():
            for c, (first, heads) in enumerate(CHUNKS):
                cols = slice(first * HD, (first + heads) * HD)
                outs[0][:, cols] = ins[8 * c + s][...]
                outs[1][:, cols] = ins[8 * c + 4 + s][0]
                outs[2][:, cols] = ins[8 * c + 4 + s][1]


def assemble(zh, parts, group, width):
    specs, args = [], []
    for dq, dkv in parts:
        for a in (*dq, *dkv):
            specs.append(pl.BlockSpec(a.shape, lambda t, z, nd=a.ndim: (0,) * nd))
            args.append(a)
    out = pl.BlockSpec((BLK, group * HD), lambda t, z: (0, lax.rem(z[0] + NZ - t, NZ)))
    return pl.pallas_call(
        assemble_body,
        grid_spec=pltpu.PrefetchScalarGridSpec(
            num_scalar_prefetch=1, grid=(NZ,), in_specs=specs, out_specs=[out] * 3
        ),
        out_shape=[jax.ShapeDtypeStruct((BLK, width), BF)] * 3,
        cost_estimate=cost(0, 6 * BLK * width * 2),
        compiler_params=grant(24),
        name="assemble",
    )(zh, *args)


def tile_bias(tile_mask, zh, slab, group):
    all_blocks, span = tile_mask.shape[1], tile_mask.shape[2]
    local = lax.dynamic_slice(tile_mask, (zh * group, slab * NZ, 0), (group, NZ, span))
    key_block = slab * NZ + jnp.arange(NZ, dtype=jnp.int32)[:, None] + jnp.arange(span, dtype=jnp.int32)[None] - span // 2
    active = (local != 0) & (key_block >= 0) & (key_block < all_blocks)
    active = active.reshape(group, 2, 2, span)
    left = jnp.pad(active[:, :, 0], ((0, 0), (0, 0), (0, 1)))
    right = jnp.pad(active[:, :, 1], ((0, 0), (0, 0), (1, 0)))
    rows = jnp.stack([left, right], -1)
    return jnp.repeat(jnp.where(rows, 0.0, -jnp.inf).astype(F32), BLK, axis=-1)


def shards(query, key, value, dout, tile_mask):
    n_ctx, n_uly = lax.axis_size("ctx"), lax.axis_size("uly")
    width = query.shape[1]
    group = tile_mask.shape[0] // NZ
    me = lax.axis_index("uly")
    zh_s = lax.rem(me, NZ)
    slab = lax.axis_index("ctx") * (n_uly // NZ) + me // NZ
    zh = zh_s.astype(jnp.int32).reshape(1)
    n_slabs = n_ctx * n_uly // NZ
    rings = [
        [(NZ * i + j, NZ * i + (j + s) % NZ) for i in range(n_uly // NZ) for j in range(NZ)] for s in range(NZ)
    ]
    up = [(NZ * i + j, NZ * (i + 1) + j) for i in range(n_slabs - 1) for j in range(NZ)]
    down = [(b, a) for a, b in up]

    def move(axes, perm, a):
        return lax.ppermute(a, axes, perm)

    def around(arrays):
        return [move("uly", rings[s], a) for s, a in enumerate(arrays, 1)]

    def to_next(a):
        return move(("ctx", "uly"), up, a)

    def to_prev(a):
        return move(("ctx", "uly"), down, a)

    key, value, query, dout = (pltpu.with_memory_space_constraint(a, pltpu.HBM) for a in (key, value, query, dout))
    bias = tile_bias(tile_mask, zh_s, slab, group)

    def gather(a, b, first, heads, wide):
        rp, rm = pack(zh, ((a, 2),), ((b, 2),), first, heads, group, wide)
        mp, mm = pack(zh, ((a, 1), (b, 1)), ((a, 3), (b, 3)), first, heads, group, wide)
        rp, rm = move("uly", rings[1], rp), move("uly", rings[3], rm)
        mp, mm = move("uly", rings[1], mp), move("uly", rings[3], mm)
        fp, fm = move("uly", rings[1], rp), move("uly", rings[3], rm)
        return mp, mm, fp, fm

    kv = gather(key, value, 0, group, group * HD // 2)
    p, m = pack(zh, ((query, 2), (query, 1), (dout, 1)), ((dout, 2), (query, 3), (dout, 3)), *CHUNKS[1], group)
    p, m = move("uly", rings[1], p), move("uly", rings[3], m)
    fp, fm = move("uly", rings[1], p[:1]), move("uly", rings[3], m[:1])
    qg = [gather(query, dout, *CHUNKS[0], CW), (p, m, fp, fm)]
    halves = unpack(zh, key, value, kv, group)
    parts = []
    for c, (first, heads) in enumerate(CHUNKS):
        recv = qg[c]
        lo, hi = halves[2 * c : 2 * c + 2]
        before, after = to_next(hi), to_prev(lo)
        *dq, rim_before, rim_after, own = attend(
            zh, query, dout, recv, before, lo, hi, after, bias, first, heads, group
        )
        from_after, from_before = to_prev(rim_before), to_next(rim_after)
        back_q = [dq[0], *around(dq[1:])]
        dkv = finish(zh, own, from_before, from_after)
        back_kv = [dkv[0], *around(dkv[1:])]
        parts.append((back_q, back_kv))
    return assemble(zh, parts, group, width)


def solution(mesh):
    rows = P(("ctx", "uly"), None)
    return jax.shard_map(
        shards,
        mesh=mesh,
        in_specs=(rows, rows, rows, rows, P()),
        out_specs=(rows, rows, rows),
        check_vma=False,
    )
```

```python
import math

import jax
import jax.numpy as jnp
from jax import lax
from jax.experimental import pallas as pl
from jax.experimental.pallas import tpu as pltpu
from jax.sharding import PartitionSpec as P


BLK = 128
HD = 128
NZ = 4
CHUNKS = ((0, 4), (4, 6))
CW = 256
SCALE = 1.0 / math.sqrt(HD)
EXP2_SCALE = SCALE / math.log(2.0)
BF = jnp.bfloat16
F32 = jnp.float32


MIB = 1 << 20


def grant(mib):
    return pltpu.CompilerParams(vmem_limit_bytes=mib * MIB)


def cost(flops, nbytes):
    return pl.CostEstimate(flops=flops, bytes_accessed=nbytes, transcendentals=0)


def pack_body(zh, *refs):
    ins, (plus, minus) = refs[:-2], refs[-2:]
    m = len(ins) // 2
    for i in range(m):
        plus[i] = ins[i][...]
        minus[i] = ins[m + i][...]


def pack(zh, plus, minus, first, heads, group, wide=CW):
    per, off, steps = group * HD // wide, first * HD // wide, heads * HD // wide
    n, m = heads * HD, len(plus)

    def src(s):
        return pl.BlockSpec((BLK, wide), lambda i, z: (0, lax.rem(z[0] + s, NZ) * per + off + i))

    out = pl.BlockSpec((m, BLK, wide), lambda i, z: (0, 0, i))
    return pl.pallas_call(
        pack_body,
        grid_spec=pltpu.PrefetchScalarGridSpec(
            num_scalar_prefetch=1,
            grid=(steps,),
            in_specs=[src(s) for _, s in (*plus, *minus)],
            out_specs=[out, out],
        ),
        out_shape=[jax.ShapeDtypeStruct((m, BLK, n), BF)] * 2,
        cost_estimate=cost(0, 4 * m * BLK * n * 2),
        compiler_params=grant(56),
    )(zh, *[a for a, _ in (*plus, *minus)])


def unpack_body(zh, k, v, mp, mm, fp, fm, *halves):
    z, step = zh[0], pl.program_id(0)
    parts = ((k, v), (mp.at[0], mp.at[1]), (fp.at[0], fm.at[0]), (mm.at[0], mm.at[1]))
    for c, (first, heads) in enumerate(CHUNKS):
        lo, hi = halves[2 * c : 2 * c + 2]

        @pl.when((step >= first * HD // CW) & (step < (first + heads) * HD // CW))
        def _():
            for s, (kk, vv) in enumerate(parts):
                b = lax.rem(z + NZ - s, NZ)

                @pl.when(b < 2)
                def _():
                    lo[b, 0] = kk[...]
                    lo[b, 1] = vv[...]

                @pl.when(b >= 2)
                def _():
                    hi[b - 2, 0] = kk[...]
                    hi[b - 2, 1] = vv[...]


def unpack(zh, k, v, recv, group):
    per = group * HD // CW
    own = pl.BlockSpec((BLK, CW), lambda i, z: (0, z[0] * per + i))
    two = pl.BlockSpec((2, BLK, CW), lambda i, z: (0, 0, i))
    one = pl.BlockSpec((1, BLK, CW), lambda i, z: (0, 0, i))
    specs, shapes = [], []
    for first, heads in CHUNKS:
        lo, n = first * HD // CW, heads * HD // CW
        half = pl.BlockSpec(
            (2, 2, BLK, CW), lambda i, z, lo=lo, n=n: (0, 0, 0, jnp.minimum(jnp.maximum(i - lo, 0), n - 1))
        )
        specs += [half, half]
        shapes += [jax.ShapeDtypeStruct((2, 2, BLK, heads * HD), BF)] * 2
    return pl.pallas_call(
        unpack_body,
        grid_spec=pltpu.PrefetchScalarGridSpec(
            num_scalar_prefetch=1, grid=(per,), in_specs=[own, own, two, two, one, one], out_specs=specs
        ),
        out_shape=shapes,
        cost_estimate=cost(0, 16 * BLK * group * HD * 2),
        compiler_params=grant(12),
        name="unpack",
    )(zh, k, v, *recv)


def attend_body(zh, q0, g0, mp, mm, fp, fm, before, lo, hi, after, bias,
                dq0, dq1, dq2, dq3, rim_before, rim_after, own,
                qs, gs, ks, vs, dqs, dk, dv):
    a = mp.shape[0] - 2
    one, two, three = (mp.at[a], mp.at[a + 1]), (fp.at[0], fm.at[0]), (mm.at[a], mm.at[a + 1])
    z = zh[0]
    for s, (qq, gg) in enumerate(((q0, g0), one, two, three)):
        row = pl.multiple_of(lax.rem(z + NZ - s, NZ) * BLK, BLK)
        qs[pl.ds(row, BLK), :] = qq[...]
        gs[pl.ds(row, BLK), :] = gg[...]
    for i, (ref, j) in enumerate(
        ((before, 0), (before, 1), (lo, 0), (lo, 1), (hi, 0), (hi, 1), (after, 0), (after, 1))
    ):
        ks[i * BLK : (i + 1) * BLK, :] = ref[j, 0]
        vs[i * BLK : (i + 1) * BLK, :] = ref[j, 1]
    nt = (((1,), (1,)), ((), ()))
    tn = (((0,), (0,)), ((), ()))
    nn = (((1,), (0,)), ((), ()))
    for pair in range(2):
        r0 = pair * 2 * BLK
        kw, vw = ks[r0 : r0 + 6 * BLK, :], vs[r0 : r0 + 6 * BLK, :]
        q, g = qs[r0 : r0 + 2 * BLK, :], gs[r0 : r0 + 2 * BLK, :]
        st = lax.dot_general(kw, q, nt, preferred_element_type=F32)
        st = st.reshape(6, BLK, 2 * BLK) + bias[0, pair][:, None, :]
        top = jnp.max(jnp.max(st, axis=0), axis=0, keepdims=True)[None]
        e = jnp.exp2((st - top) * EXP2_SCALE)
        total = jnp.sum(jnp.sum(e, axis=0), axis=0, keepdims=True)[None]
        p = e * (1.0 / total)
        dp = lax.dot_general(vw, g, nt, preferred_element_type=F32).reshape(6, BLK, 2 * BLK)
        delta = jnp.sum(jnp.sum(p * dp, axis=0), axis=0, keepdims=True)[None]
        ds = (p * (dp - delta)).astype(BF).reshape(6 * BLK, 2 * BLK)
        pb = p.astype(BF).reshape(6 * BLK, 2 * BLK)
        dvw = lax.dot_general(pb, g, nn, preferred_element_type=F32)
        dkw = lax.dot_general(ds, q, nn, preferred_element_type=F32)
        dqw = lax.dot_general(ds, kw, tn, preferred_element_type=F32) * SCALE
        dqs[2 * pair] = dqw[:BLK].astype(BF)
        dqs[2 * pair + 1] = dqw[BLK:].astype(BF)
        if pair == 0:
            dk[: 6 * BLK, :] = dkw
            dv[: 6 * BLK, :] = dvw
        else:
            dk[2 * BLK : 6 * BLK, :] += dkw[: 4 * BLK]
            dv[2 * BLK : 6 * BLK, :] += dvw[: 4 * BLK]
            dk[6 * BLK :, :] = dkw[4 * BLK :]
            dv[6 * BLK :, :] = dvw[4 * BLK :]
    for s, o in enumerate((dq0, dq1, dq2, dq3)):
        o[...] = dqs[lax.rem(z + s, NZ)]
    for j in range(2):
        rim_before[j, 0] = (dk[j * BLK : (j + 1) * BLK, :] * SCALE).astype(BF)
        rim_before[j, 1] = dv[j * BLK : (j + 1) * BLK, :].astype(BF)
        rim_after[j, 0] = (dk[(6 + j) * BLK : (7 + j) * BLK, :] * SCALE).astype(BF)
        rim_after[j, 1] = dv[(6 + j) * BLK : (7 + j) * BLK, :].astype(BF)
    for j in range(4):
        own[j, 0] = dk[(2 + j) * BLK : (3 + j) * BLK, :] * SCALE
        own[j, 1] = dv[(2 + j) * BLK : (3 + j) * BLK, :]


def attend(zh, q, g, recv, before, lo, hi, after, bias, first, heads, group):
    n = heads * HD
    mine = pl.BlockSpec((BLK, HD), lambda h, z: (0, z[0] * group + first + h))
    got = [pl.BlockSpec((a.shape[0], BLK, HD), lambda h, z: (0, 0, h)) for a in recv]
    flat = pl.BlockSpec((BLK, HD), lambda h, z: (0, h))
    rim = pl.BlockSpec((2, 2, BLK, HD), lambda h, z: (0, 0, 0, h))
    own = pl.BlockSpec((4, 2, BLK, HD), lambda h, z: (0, 0, 0, h))
    shape = jax.ShapeDtypeStruct
    return pl.pallas_call(
        attend_body,
        grid_spec=pltpu.PrefetchScalarGridSpec(
            num_scalar_prefetch=1,
            grid=(heads,),
            in_specs=[mine, mine, *got, rim, rim, rim, rim,
                      pl.BlockSpec((1, 2, 6, 2 * BLK), lambda h, z: (first + h, 0, 0, 0))],
            out_specs=[flat] * 4 + [rim, rim, own],
            scratch_shapes=[
                pltpu.VMEM((4 * BLK, HD), BF),
                pltpu.VMEM((4 * BLK, HD), BF),
                pltpu.VMEM((8 * BLK, HD), BF),
                pltpu.VMEM((8 * BLK, HD), BF),
                pltpu.VMEM((4, BLK, HD), BF),
                pltpu.VMEM((8 * BLK, HD), F32),
                pltpu.VMEM((8 * BLK, HD), F32),
            ],
        ),
        out_shape=[shape((BLK, n), BF)] * 4
        + [shape((2, 2, BLK, n), BF)] * 2
        + [shape((4, 2, BLK, n), F32)],
        cost_estimate=cost(heads * 2 * 5 * 2 * 768 * 256 * 128, 40 * BLK * n * 2),
        compiler_params=grant(24),
    )(zh, q, g, *recv, before, lo, hi, after, bias)


def finish_body(zh, own, before, before_seam, after, after_seam, o0, o1, o2, o3):
    z = zh[0]
    for s, o in enumerate((o0, o1, o2, o3)):
        b = lax.rem(z + s, NZ)

        @pl.when(b < 2)
        def _():
            o[...] = (own[b] + (before[b].astype(F32) + before_seam[b].astype(F32))).astype(BF)

        @pl.when(b >= 2)
        def _():
            o[...] = (own[b] + (after[b - 2].astype(F32) + after_seam[b - 2].astype(F32))).astype(BF)


def finish(zh, own, from_before, from_after):
    n = own.shape[-1]
    rim = pl.BlockSpec((2, 2, BLK, CW), lambda i, z: (0, 0, 0, i))
    out = pl.BlockSpec((2, BLK, CW), lambda i, z: (0, 0, i))
    return pl.pallas_call(
        finish_body,
        grid_spec=pltpu.PrefetchScalarGridSpec(
            num_scalar_prefetch=1,
            grid=(n // CW,),
            in_specs=[pl.BlockSpec((4, 2, BLK, CW), lambda i, z: (0, 0, 0, i)), rim, rim, rim, rim],
            out_specs=[out] * 4,
        ),
        out_shape=[jax.ShapeDtypeStruct((2, BLK, n), BF)] * 4,
        cost_estimate=cost(0, 32 * BLK * n * 2),
        compiler_params=grant(14),
    )(zh, own, *from_before, *from_after)


def assemble_body(zh, *refs):
    n_chunks = len(CHUNKS)
    ins, outs = refs[: 8 * n_chunks], refs[8 * n_chunks :]
    t = pl.program_id(0)
    for s in range(NZ):

        @pl.when(t == s)
        def _():
            for c, (first, heads) in enumerate(CHUNKS):
                cols = slice(first * HD, (first + heads) * HD)
                outs[0][:, cols] = ins[8 * c + s][...]
                outs[1][:, cols] = ins[8 * c + 4 + s][0]
                outs[2][:, cols] = ins[8 * c + 4 + s][1]


def assemble(zh, parts, group, width):
    specs, args = [], []
    for dq, dkv in parts:
        for a in (*dq, *dkv):
            specs.append(pl.BlockSpec(a.shape, lambda t, z, nd=a.ndim: (0,) * nd))
            args.append(a)
    out = pl.BlockSpec((BLK, group * HD), lambda t, z: (0, lax.rem(z[0] + NZ - t, NZ)))
    return pl.pallas_call(
        assemble_body,
        grid_spec=pltpu.PrefetchScalarGridSpec(
            num_scalar_prefetch=1, grid=(NZ,), in_specs=specs, out_specs=[out] * 3
        ),
        out_shape=[jax.ShapeDtypeStruct((BLK, width), BF)] * 3,
        cost_estimate=cost(0, 6 * BLK * width * 2),
        compiler_params=grant(24),
        name="assemble",
    )(zh, *args)


def tile_bias(tile_mask, zh, slab, group):
    all_blocks, span = tile_mask.shape[1], tile_mask.shape[2]
    local = lax.dynamic_slice(tile_mask, (zh * group, slab * NZ, 0), (group, NZ, span))
    key_block = slab * NZ + jnp.arange(NZ, dtype=jnp.int32)[:, None] + jnp.arange(span, dtype=jnp.int32)[None] - span // 2
    active = (local != 0) & (key_block >= 0) & (key_block < all_blocks)
    active = active.reshape(group, 2, 2, span)
    left = jnp.pad(active[:, :, 0], ((0, 0), (0, 0), (0, 1)))
    right = jnp.pad(active[:, :, 1], ((0, 0), (0, 0), (1, 0)))
    rows = jnp.stack([left, right], -1)
    return jnp.repeat(jnp.where(rows, 0.0, -jnp.inf).astype(F32), BLK, axis=-1)


def shards(query, key, value, dout, tile_mask):
    n_ctx, n_uly = lax.axis_size("ctx"), lax.axis_size("uly")
    width = query.shape[1]
    group = tile_mask.shape[0] // NZ
    me = lax.axis_index("uly")
    zh_s = lax.rem(me, NZ)
    slab = lax.axis_index("ctx") * (n_uly // NZ) + me // NZ
    zh = zh_s.astype(jnp.int32).reshape(1)
    n_slabs = n_ctx * n_uly // NZ
    rings = [
        [(NZ * i + j, NZ * i + (j + s) % NZ) for i in range(n_uly // NZ) for j in range(NZ)] for s in range(NZ)
    ]
    up = [(NZ * i + j, NZ * (i + 1) + j) for i in range(n_slabs - 1) for j in range(NZ)]
    down = [(b, a) for a, b in up]
    seam = n_slabs // 2 - 1
    low, high = ([NZ * (seam + i) + j for j in range(NZ)] for i in range(2))
    via_up = [3 * n_uly + NZ + j for j in range(NZ)]
    via_down = [12 * n_uly + 2 * NZ + j for j in range(NZ)]

    def move(axes, perm, a):
        return lax.ppermute(a, axes, perm)

    def around(arrays):
        return [move("uly", rings[s], a) for s, a in enumerate(arrays, 1)]

    def to_next(a):
        return move(("ctx", "uly"), up, a)

    def to_prev(a):
        return move(("ctx", "uly"), down, a)

    def rim_move(perm, first, via, last, a):
        both = ("ctx", "uly")
        direct = move(both, [p for p in perm if p[0] not in first], a)
        hop = move(both, list(zip(first, via)), a)
        return direct, move(both, list(zip(via, last)), hop)

    key, value, query, dout = (pltpu.with_memory_space_constraint(a, pltpu.HBM) for a in (key, value, query, dout))
    bias = tile_bias(tile_mask, zh_s, slab, group)

    def gather(a, b, first, heads, wide):
        rp, rm = pack(zh, ((a, 2),), ((b, 2),), first, heads, group, wide)
        mp, mm = pack(zh, ((a, 1), (b, 1)), ((a, 3), (b, 3)), first, heads, group, wide)
        rp, rm = move("uly", rings[1], rp), move("uly", rings[3], rm)
        mp, mm = move("uly", rings[1], mp), move("uly", rings[3], mm)
        fp, fm = move("uly", rings[1], rp), move("uly", rings[3], rm)
        return mp, mm, fp, fm

    kv = gather(key, value, 0, group, group * HD // 2)
    p, m = pack(zh, ((query, 2), (query, 1), (dout, 1)), ((dout, 2), (query, 3), (dout, 3)), *CHUNKS[1], group)
    p, m = move("uly", rings[1], p), move("uly", rings[3], m)
    fp, fm = move("uly", rings[1], p[:1]), move("uly", rings[3], m[:1])
    qg = [gather(query, dout, *CHUNKS[0], CW), (p, m, fp, fm)]
    halves = unpack(zh, key, value, kv, group)
    parts = []
    for c, (first, heads) in enumerate(CHUNKS):
        recv = qg[c]
        lo, hi = halves[2 * c : 2 * c + 2]
        before, after = to_next(hi), to_prev(lo)
        *dq, rim_before, rim_after, own = attend(
            zh, query, dout, recv, before, lo, hi, after, bias, first, heads, group
        )
        from_after = rim_move(down, high, via_down, low, rim_before)
        from_before = rim_move(up, low, via_up, high, rim_after)
        back_q = [dq[0], *around(dq[1:])]
        dkv = finish(zh, own, from_before, from_after)
        back_kv = [dkv[0], *around(dkv[1:])]
        parts.append((back_q, back_kv))
    return assemble(zh, parts, group, width)


def solution(mesh):
    rows = P(("ctx", "uly"), None)
    return jax.shard_map(
        shards,
        mesh=mesh,
        in_specs=(rows, rows, rows, rows, P()),
        out_specs=(rows, rows, rows),
        check_vma=False,
    )
```

```python
import math

import jax
import jax.numpy as jnp
from jax import lax
from jax.experimental import pallas as pl
from jax.experimental.pallas import tpu as pltpu
from jax.sharding import PartitionSpec as P


BLK = 128
HD = 128
NZ = 4
CHUNKS = ((0, 4), (4, 6))
CW = 256
SCALE = 1.0 / math.sqrt(HD)
EXP2_SCALE = SCALE / math.log(2.0)
BF = jnp.bfloat16
F32 = jnp.float32


MIB = 1 << 20


def grant(mib):
    return pltpu.CompilerParams(vmem_limit_bytes=mib * MIB)


def cost(flops, nbytes):
    return pl.CostEstimate(flops=flops, bytes_accessed=nbytes, transcendentals=0)


def pack_body(zh, *refs):
    ins, (plus, minus) = refs[:-2], refs[-2:]
    m = len(ins) // 2
    for i in range(m):
        plus[i] = ins[i][...]
        minus[i] = ins[m + i][...]


def pack(zh, plus, minus, first, heads, group, wide=CW):
    per, off, steps = group * HD // wide, first * HD // wide, heads * HD // wide
    n, m = heads * HD, len(plus)

    def src(s):
        return pl.BlockSpec((BLK, wide), lambda i, z: (0, lax.rem(z[0] + s, NZ) * per + off + i))

    out = pl.BlockSpec((m, BLK, wide), lambda i, z: (0, 0, i))
    return pl.pallas_call(
        pack_body,
        grid_spec=pltpu.PrefetchScalarGridSpec(
            num_scalar_prefetch=1,
            grid=(steps,),
            in_specs=[src(s) for _, s in (*plus, *minus)],
            out_specs=[out, out],
        ),
        out_shape=[jax.ShapeDtypeStruct((m, BLK, n), BF)] * 2,
        cost_estimate=cost(0, 4 * m * BLK * n * 2),
        compiler_params=grant(56),
    )(zh, *[a for a, _ in (*plus, *minus)])


def unpack_body(zh, k, v, mp, mm, fp, fm, *halves):
    z, step = zh[0], pl.program_id(0)
    parts = ((k, v), (mp.at[0], mp.at[1]), (fp.at[0], fm.at[0]), (mm.at[0], mm.at[1]))
    for c, (first, heads) in enumerate(CHUNKS):
        lo, hi = halves[2 * c : 2 * c + 2]

        @pl.when((step >= first * HD // CW) & (step < (first + heads) * HD // CW))
        def _():
            for s, (kk, vv) in enumerate(parts):
                b = lax.rem(z + NZ - s, NZ)

                @pl.when(b < 2)
                def _():
                    lo[b, 0] = kk[...]
                    lo[b, 1] = vv[...]

                @pl.when(b >= 2)
                def _():
                    hi[b - 2, 0] = kk[...]
                    hi[b - 2, 1] = vv[...]


def unpack(zh, k, v, recv, group):
    per = group * HD // CW
    own = pl.BlockSpec((BLK, CW), lambda i, z: (0, z[0] * per + i))
    two = pl.BlockSpec((2, BLK, CW), lambda i, z: (0, 0, i))
    one = pl.BlockSpec((1, BLK, CW), lambda i, z: (0, 0, i))
    specs, shapes = [], []
    for first, heads in CHUNKS:
        lo, n = first * HD // CW, heads * HD // CW
        half = pl.BlockSpec(
            (2, 2, BLK, CW), lambda i, z, lo=lo, n=n: (0, 0, 0, jnp.minimum(jnp.maximum(i - lo, 0), n - 1))
        )
        specs += [half, half]
        shapes += [jax.ShapeDtypeStruct((2, 2, BLK, heads * HD), BF)] * 2
    return pl.pallas_call(
        unpack_body,
        grid_spec=pltpu.PrefetchScalarGridSpec(
            num_scalar_prefetch=1, grid=(per,), in_specs=[own, own, two, two, one, one], out_specs=specs
        ),
        out_shape=shapes,
        cost_estimate=cost(0, 16 * BLK * group * HD * 2),
        compiler_params=grant(12),
        name="unpack",
    )(zh, k, v, *recv)


def attend_body(zh, q0, g0, mp, mm, fp, fm, before, lo, hi, after, bias,
                dq0, dq1, dq2, dq3, rim_before, rim_after, own,
                qs, gs, ks, vs, dqs, dk, dv):
    a = mp.shape[0] - 2
    one, two, three = (mp.at[a], mp.at[a + 1]), (fp.at[0], fm.at[0]), (mm.at[a], mm.at[a + 1])
    z = zh[0]
    for s, (qq, gg) in enumerate(((q0, g0), one, two, three)):
        row = pl.multiple_of(lax.rem(z + NZ - s, NZ) * BLK, BLK)
        qs[pl.ds(row, BLK), :] = qq[...]
        gs[pl.ds(row, BLK), :] = gg[...]
    for i, (ref, j) in enumerate(
        ((before, 0), (before, 1), (lo, 0), (lo, 1), (hi, 0), (hi, 1), (after, 0), (after, 1))
    ):
        ks[i * BLK : (i + 1) * BLK, :] = ref[j, 0]
        vs[i * BLK : (i + 1) * BLK, :] = ref[j, 1]
    nt = (((1,), (1,)), ((), ()))
    tn = (((0,), (0,)), ((), ()))
    nn = (((1,), (0,)), ((), ()))
    for pair in range(2):
        r0 = pair * 2 * BLK
        kw, vw = ks[r0 : r0 + 6 * BLK, :], vs[r0 : r0 + 6 * BLK, :]
        q, g = qs[r0 : r0 + 2 * BLK, :], gs[r0 : r0 + 2 * BLK, :]
        st = lax.dot_general(kw, q, nt, preferred_element_type=F32)
        st = st.reshape(6, BLK, 2 * BLK) + bias[0, pair][:, None, :]
        top = jnp.max(jnp.max(st, axis=0), axis=0, keepdims=True)[None]
        e = jnp.exp2((st - top) * EXP2_SCALE)
        total = jnp.sum(jnp.sum(e, axis=0), axis=0, keepdims=True)[None]
        p = e * (1.0 / total)
        dp = lax.dot_general(vw, g, nt, preferred_element_type=F32).reshape(6, BLK, 2 * BLK)
        delta = jnp.sum(jnp.sum(p * dp, axis=0), axis=0, keepdims=True)[None]
        ds = (p * (dp - delta)).astype(BF).reshape(6 * BLK, 2 * BLK)
        pb = p.astype(BF).reshape(6 * BLK, 2 * BLK)
        dvw = lax.dot_general(pb, g, nn, preferred_element_type=F32)
        dkw = lax.dot_general(ds, q, nn, preferred_element_type=F32)
        dqw = lax.dot_general(ds, kw, tn, preferred_element_type=F32) * SCALE
        dqs[2 * pair] = dqw[:BLK].astype(BF)
        dqs[2 * pair + 1] = dqw[BLK:].astype(BF)
        if pair == 0:
            dk[: 6 * BLK, :] = dkw
            dv[: 6 * BLK, :] = dvw
        else:
            dk[2 * BLK : 6 * BLK, :] += dkw[: 4 * BLK]
            dv[2 * BLK : 6 * BLK, :] += dvw[: 4 * BLK]
            dk[6 * BLK :, :] = dkw[4 * BLK :]
            dv[6 * BLK :, :] = dvw[4 * BLK :]
    for s, o in enumerate((dq0, dq1, dq2, dq3)):
        o[...] = dqs[lax.rem(z + s, NZ)]
    for j in range(2):
        rim_before[j, 0] = (dk[j * BLK : (j + 1) * BLK, :] * SCALE).astype(BF)
        rim_before[j, 1] = dv[j * BLK : (j + 1) * BLK, :].astype(BF)
        rim_after[j, 0] = (dk[(6 + j) * BLK : (7 + j) * BLK, :] * SCALE).astype(BF)
        rim_after[j, 1] = dv[(6 + j) * BLK : (7 + j) * BLK, :].astype(BF)
    for j in range(4):
        own[j, 0] = dk[(2 + j) * BLK : (3 + j) * BLK, :] * SCALE
        own[j, 1] = dv[(2 + j) * BLK : (3 + j) * BLK, :]


def attend(zh, q, g, recv, before, lo, hi, after, bias, first, heads, group):
    n = heads * HD
    mine = pl.BlockSpec((BLK, HD), lambda h, z: (0, z[0] * group + first + h))
    got = [pl.BlockSpec((a.shape[0], BLK, HD), lambda h, z: (0, 0, h)) for a in recv]
    flat = pl.BlockSpec((BLK, HD), lambda h, z: (0, h))
    rim = pl.BlockSpec((2, 2, BLK, HD), lambda h, z: (0, 0, 0, h))
    own = pl.BlockSpec((4, 2, BLK, HD), lambda h, z: (0, 0, 0, h))
    shape = jax.ShapeDtypeStruct
    return pl.pallas_call(
        attend_body,
        grid_spec=pltpu.PrefetchScalarGridSpec(
            num_scalar_prefetch=1,
            grid=(heads,),
            in_specs=[mine, mine, *got, rim, rim, rim, rim,
                      pl.BlockSpec((1, 2, 6, 2 * BLK), lambda h, z: (first + h, 0, 0, 0))],
            out_specs=[flat] * 4 + [rim, rim, own],
            scratch_shapes=[
                pltpu.VMEM((4 * BLK, HD), BF),
                pltpu.VMEM((4 * BLK, HD), BF),
                pltpu.VMEM((8 * BLK, HD), BF),
                pltpu.VMEM((8 * BLK, HD), BF),
                pltpu.VMEM((4, BLK, HD), BF),
                pltpu.VMEM((8 * BLK, HD), F32),
                pltpu.VMEM((8 * BLK, HD), F32),
            ],
        ),
        out_shape=[shape((BLK, n), BF)] * 4
        + [shape((2, 2, BLK, n), BF)] * 2
        + [shape((4, 2, BLK, n), F32)],
        cost_estimate=cost(heads * 2 * 5 * 2 * 768 * 256 * 128, 40 * BLK * n * 2),
        compiler_params=grant(24),
    )(zh, q, g, *recv, before, lo, hi, after, bias)


def finish_body(zh, own, *refs):
    n = (len(refs) - NZ) // 2
    before, after, outs = refs[:n], refs[n : 2 * n], refs[2 * n :]
    z = zh[0]
    for s, o in enumerate(outs):
        b = lax.rem(z + s, NZ)

        @pl.when(b < 2)
        def _():
            o[...] = (own[b] + sum(r[b].astype(F32) for r in before)).astype(BF)

        @pl.when(b >= 2)
        def _():
            o[...] = (own[b] + sum(r[b - 2].astype(F32) for r in after)).astype(BF)


def finish(zh, own, from_before, from_after):
    n = own.shape[-1]
    rim = pl.BlockSpec((2, 2, BLK, CW), lambda i, z: (0, 0, 0, i))
    out = pl.BlockSpec((2, BLK, CW), lambda i, z: (0, 0, i))
    return pl.pallas_call(
        finish_body,
        grid_spec=pltpu.PrefetchScalarGridSpec(
            num_scalar_prefetch=1,
            grid=(n // CW,),
            in_specs=[pl.BlockSpec((4, 2, BLK, CW), lambda i, z: (0, 0, 0, i))] + [rim] * (2 * len(from_before)),
            out_specs=[out] * 4,
        ),
        out_shape=[jax.ShapeDtypeStruct((2, BLK, n), BF)] * 4,
        cost_estimate=cost(0, 32 * BLK * n * 2),
        compiler_params=grant(14),
    )(zh, own, *from_before, *from_after)


def assemble_body(zh, *refs):
    n_chunks = len(CHUNKS)
    ins, outs = refs[: 8 * n_chunks], refs[8 * n_chunks :]
    t = pl.program_id(0)
    for s in range(NZ):

        @pl.when(t == s)
        def _():
            for c, (first, heads) in enumerate(CHUNKS):
                cols = slice(first * HD, (first + heads) * HD)
                outs[0][:, cols] = ins[8 * c + s][...]
                outs[1][:, cols] = ins[8 * c + 4 + s][0]
                outs[2][:, cols] = ins[8 * c + 4 + s][1]


def assemble(zh, parts, group, width):
    specs, args = [], []
    for dq, dkv in parts:
        for a in (*dq, *dkv):
            specs.append(pl.BlockSpec(a.shape, lambda t, z, nd=a.ndim: (0,) * nd))
            args.append(a)
    out = pl.BlockSpec((BLK, group * HD), lambda t, z: (0, lax.rem(z[0] + NZ - t, NZ)))
    return pl.pallas_call(
        assemble_body,
        grid_spec=pltpu.PrefetchScalarGridSpec(
            num_scalar_prefetch=1, grid=(NZ,), in_specs=specs, out_specs=[out] * 3
        ),
        out_shape=[jax.ShapeDtypeStruct((BLK, width), BF)] * 3,
        cost_estimate=cost(0, 6 * BLK * width * 2),
        compiler_params=grant(24),
        name="assemble",
    )(zh, *args)


def tile_bias(tile_mask, zh, slab, group):
    all_blocks, span = tile_mask.shape[1], tile_mask.shape[2]
    local = lax.dynamic_slice(tile_mask, (zh * group, slab * NZ, 0), (group, NZ, span))
    key_block = slab * NZ + jnp.arange(NZ, dtype=jnp.int32)[:, None] + jnp.arange(span, dtype=jnp.int32)[None] - span // 2
    active = (local != 0) & (key_block >= 0) & (key_block < all_blocks)
    active = active.reshape(group, 2, 2, span)
    left = jnp.pad(active[:, :, 0], ((0, 0), (0, 0), (0, 1)))
    right = jnp.pad(active[:, :, 1], ((0, 0), (0, 0), (1, 0)))
    rows = jnp.stack([left, right], -1)
    return jnp.repeat(jnp.where(rows, 0.0, -jnp.inf).astype(F32), BLK, axis=-1)


def shards(query, key, value, dout, tile_mask):
    n_ctx, n_uly = lax.axis_size("ctx"), lax.axis_size("uly")
    width = query.shape[1]
    group = tile_mask.shape[0] // NZ
    me = lax.axis_index("uly")
    zh_s = lax.rem(me, NZ)
    slab = lax.axis_index("ctx") * (n_uly // NZ) + me // NZ
    zh = zh_s.astype(jnp.int32).reshape(1)
    n_slabs = n_ctx * n_uly // NZ
    rings = [
        [(NZ * i + j, NZ * i + (j + s) % NZ) for i in range(n_uly // NZ) for j in range(NZ)] for s in range(NZ)
    ]
    up = [(NZ * i + j, NZ * (i + 1) + j) for i in range(n_slabs - 1) for j in range(NZ)]
    down = [(b, a) for a, b in up]
    seam = n_slabs // 2 - 1
    low, high = ([NZ * (seam + i) + j for j in range(NZ)] for i in range(2))
    via_up = [3 * n_uly + NZ + j for j in range(NZ)]
    via_down = [12 * n_uly + 2 * NZ + j for j in range(NZ)]

    def move(axes, perm, a):
        return lax.ppermute(a, axes, perm)

    def around(arrays):
        return [move("uly", rings[s], a) for s, a in enumerate(arrays, 1)]

    def to_next(a):
        return move(("ctx", "uly"), up, a)

    def to_prev(a):
        return move(("ctx", "uly"), down, a)

    def rim_move(perm, first, via, last, a):
        both = ("ctx", "uly")
        direct = move(both, [p for p in perm if p[0] not in first], a)
        hop = move(both, list(zip(first, via)), a)
        return direct, move(both, list(zip(via, last)), hop)

    key, value, query, dout = (pltpu.with_memory_space_constraint(a, pltpu.HBM) for a in (key, value, query, dout))
    bias = tile_bias(tile_mask, zh_s, slab, group)

    def gather(a, b, first, heads, wide):
        rp, rm = pack(zh, ((a, 2),), ((b, 2),), first, heads, group, wide)
        mp, mm = pack(zh, ((a, 1), (b, 1)), ((a, 3), (b, 3)), first, heads, group, wide)
        rp, rm = move("uly", rings[1], rp), move("uly", rings[3], rm)
        mp, mm = move("uly", rings[1], mp), move("uly", rings[3], mm)
        fp, fm = move("uly", rings[1], rp), move("uly", rings[3], rm)
        return mp, mm, fp, fm

    kv = gather(key, value, 0, group, group * HD // 2)
    p, m = pack(zh, ((query, 2), (query, 1), (dout, 1)), ((dout, 2), (query, 3), (dout, 3)), *CHUNKS[1], group)
    p, m = move("uly", rings[1], p), move("uly", rings[3], m)
    fp, fm = move("uly", rings[1], p[:1]), move("uly", rings[3], m[:1])
    qg = [gather(query, dout, *CHUNKS[0], CW), (p, m, fp, fm)]
    halves = unpack(zh, key, value, kv, group)
    parts = []
    for c, (first, heads) in enumerate(CHUNKS):
        recv = qg[c]
        lo, hi = halves[2 * c : 2 * c + 2]
        before, after = to_next(hi), to_prev(lo)
        *dq, rim_before, rim_after, own = attend(
            zh, query, dout, recv, before, lo, hi, after, bias, first, heads, group
        )
        if c == 0:
            from_after = rim_move(down, high, via_down, low, rim_before)
            from_before = rim_move(up, low, via_up, high, rim_after)
        else:
            from_after, from_before = (to_prev(rim_before),), (to_next(rim_after),)
        back_q = [dq[0], *around(dq[1:])]
        dkv = finish(zh, own, from_before, from_after)
        back_kv = [dkv[0], *around(dkv[1:])]
        parts.append((back_q, back_kv))
    return assemble(zh, parts, group, width)


def solution(mesh):
    rows = P(("ctx", "uly"), None)
    return jax.shard_map(
        shards,
        mesh=mesh,
        in_specs=(rows, rows, rows, rows, P()),
        out_specs=(rows, rows, rows),
        check_vma=False,
    )
```
